32 devices in a mesh: grid: 8 (over z, y), tile: 4 (over x, core).
Axes of the slice: x: 2, y: 2, z: 4, core: 2. Of those that a mesh axis runs over, the one named last changes fastest.
Arguments:
- point_values: bfloat16 [256, 16384], P('grid', 'tile'), may hold values from -1.75 to 1.75
- sig_blocks: int32 [8, 16], P('grid'), may hold values from 0 to 31, as said below
- density: bfloat16 [16384, 16384], P('grid', 'tile'), may hold values from -0.0625 to 0.0625
- coulomb_core: bfloat16 [512, 512], replicated, may hold values from -0.25 to 0.25
- screen_mask: int32 [32, 32], replicated, may hold values 0 or 1
- ao_centers: float32 [3, 16384], replicated, may hold values from -1 to 1
- ao_widths: float32 [16384], replicated, may hold values from 0.25 to 1
- point_coords: float32 [3, 256], P(None, 'grid'), may hold values from -1 to 1
- lmo_coeffs: bfloat16 [16384, 1024], P('tile'), may hold values from -0.0625 to 0.0625
- domain_blocks: int32 [4, 16], replicated, may hold values from 0 to 31, as said below
Outputs:
- half: bfloat16 [1024, 16384], P('tile', 'grid')
The draws below stay inside these ranges and needn't reach their ends.
Inputs may be any that keep to these rules, and one draw needn't show every extreme that they name: `sig_blocks`: each batch names 16 different AO blocks. `domain_blocks`: each strip's 16 blocks are different, and every AO block lies in the domain of some strip.
All inputs are finite; a program needn't handle non-finite values.
Results may differ from the reference program's by a relative error of at most 0.02.
Values may be sent and summed in bfloat16 or wider, within the bound.
A program may use at most 128 MiB of HBM per device.

```python
import math
import jax
import jax.numpy as jnp
from jax import lax

NAO = 16384
BLK = 512
BP = 32
LSTRIP = 256
DOMN = 16
BASIS_GROUP_NUM = 32
SIGN = 16
NBATCH = 8
POINTS = 256
CT = 4096
NSTRIP = 4
NLMO = 1024
N_TILE = 4


def draw_sig_blocks(key, part):
    preferred_sequence = jax.random.permutation(jax.random.fold_in(key, 7), BASIS_GROUP_NUM)
    preference_increment = jnp.where(preferred_sequence < 4, 512, 0)
    raw_ranking_weights = jax.random.randint(jax.random.fold_in(key, 8), (NBATCH, BASIS_GROUP_NUM), 0, 1024)
    group_ranking_weights = (raw_ranking_weights + preference_increment[None, :]) * BASIS_GROUP_NUM + jnp.arange(BASIS_GROUP_NUM, dtype=jnp.int32)[None, :]
    return lax.top_k(group_ranking_weights, SIGN)[1].astype(jnp.int32)


def draw_domain_blocks(key, part):
    shuffled = jax.random.permutation(jax.random.fold_in(key, 9), BASIS_GROUP_NUM)
    window_starts = jnp.arange(NSTRIP, dtype=jnp.int32) * (BASIS_GROUP_NUM // NSTRIP)
    positions = (window_starts[:, None] + jnp.arange(DOMN, dtype=jnp.int32)[None, :]) % BASIS_GROUP_NUM
    return shuffled[positions].astype(jnp.int32)


def set_ends(drawn, own_key, low, largest):
    shape = drawn.shape
    place = [jax.random.randint(jax.random.fold_in(own_key, axis), (), 0, shape[axis]) for axis in range(len(shape))]
    drawn = drawn.at[tuple(place)].set(low)
    longest = shape.index(max(shape))
    place[longest] = (place[longest] + 1) % shape[longest]
    return drawn.at[tuple(place)].set(largest)


def block_scale(stream_key, extent, shards, low, high):
    factor_of = 1.0
    for position, parts in shards:
        draws = jax.random.uniform(jax.random.fold_in(jax.random.fold_in(stream_key, 6), position), (parts,), jnp.float32, low / len(shards), high / len(shards))
        factor_of = factor_of * jnp.repeat(jnp.exp(draws), extent[position] // parts).reshape((-1,) + (1,) * (len(extent) - 1 - position))
    return factor_of


def scatter_about(key, dims, width, bound, cuts=(), kind=jnp.bfloat16):
    result = width * jax.random.normal(key, dims, jnp.float32)
    if cuts:
        result = result * block_scale(key, dims, cuts, -0.22, 0.18)
    return jnp.clip(result, -bound, bound).astype(kind)


def setup_inputs(seed: int = 0) -> dict:
    seeds = jax.random.split(jax.random.key(seed), 11)
    return {
        "point_values": scatter_about(seeds[0], (POINTS, NAO), 0.3, 1.75, ((0, 8), (1, 4))),
        "sig_blocks": draw_sig_blocks(jax.random.fold_in(seeds[10], 71), 0),
        "density": scatter_about(seeds[2], (NAO, NAO), (SIGN * BLK) ** -0.5, 0.0625, ((0, 8), (1, 4))),
        "coulomb_core": scatter_about(seeds[3], (BLK, BLK), BLK ** -0.5, 0.25),
        "screen_mask": set_ends((jax.random.randint(seeds[4], (BASIS_GROUP_NUM, BASIS_GROUP_NUM), 0, 4) < 3).astype(jnp.int32), jax.random.fold_in(seeds[4], 1), 0, 1),
        "ao_centers": jnp.clip(jax.random.uniform(seeds[5], (3, NAO), jnp.float32, -1.0, 1.0), -1.0, 1.0),
        "ao_widths": jnp.clip(jnp.exp(jax.random.uniform(seeds[6], (NAO,), jnp.float32, math.log(0.25), math.log(1.0))), 0.25, 1.0),
        "point_coords": jnp.clip(jax.random.uniform(seeds[7], (3, POINTS), jnp.float32, -1.0, 1.0) * block_scale(seeds[7], (3, POINTS), ((1, 8),), -0.4, 0.0), -1.0, 1.0),
        "lmo_coeffs": scatter_about(seeds[8], (NAO, NLMO), (DOMN * BLK) ** -0.5, 0.0625, ((0, 4),)),
        "domain_blocks": draw_domain_blocks(jax.random.fold_in(seeds[10], 71), 0),
    }


highest = lax.Precision.HIGHEST

def batch_factors(values, block_list, coords, density_blocks, coulomb_core, screen_mask, ao_centers, ao_widths):
    sig_density = density_blocks[block_list][:, :, block_list, :].astype(jnp.float32)
    sig_values = values.reshape(BP, BASIS_GROUP_NUM, BLK)[:, block_list, :]
    per_column = jnp.einsum('kajc,pjc->jpka', sig_density, sig_values.astype(jnp.float32), precision=highest)
    owners = block_list // (CT // BLK)
    owner_onehot = (owners[:, None] == jnp.arange(N_TILE, dtype=jnp.int32)[None, :]).astype(jnp.float32)
    by_tile = jnp.einsum('jt,jpka->tpka', owner_onehot, per_column, precision=highest)
    rounded = lax.optimization_barrier(by_tile.astype(jnp.bfloat16)).astype(jnp.float32)
    density_term = lax.optimization_barrier(jnp.sum(rounded, axis=0))
    offsets = ao_centers[:, None, :] - coords[:, :, None]
    coefficient = 1.0 / jnp.sqrt(lax.optimization_barrier(jnp.sum(offsets * offsets, axis=0)) + ao_widths[None, :])
    sig_coeff = coefficient.reshape(BP, BASIS_GROUP_NUM, BLK)[:, block_list, :]
    weighted = sig_coeff * density_term
    screen = screen_mask[block_list][:, block_list].astype(jnp.float32)
    screened = jnp.einsum('kj,pja->pka', screen, weighted, precision=highest)
    mixed_term = jnp.einsum('ab,pkb->pka', coulomb_core.astype(jnp.float32), screened, precision=highest)
    potential = (sig_coeff * mixed_term).astype(jnp.bfloat16)
    return (sig_values, potential)

def reference(point_values, sig_blocks, density, coulomb_core, screen_mask, ao_centers, ao_widths, point_coords, lmo_coeffs, domain_blocks):
    density_blocks = density.reshape(BASIS_GROUP_NUM, BLK, BASIS_GROUP_NUM, BLK)
    values = point_values.reshape(NBATCH, BP, NAO)
    coords = jnp.transpose(point_coords.reshape(3, NBATCH, BP), (1, 0, 2))

    def one_batch(entries):
        return batch_factors(entries[0], entries[1], entries[2], density_blocks, coulomb_core, screen_mask, ao_centers, ao_widths)
    sig_values, potentials = lax.map(one_batch, (values, sig_blocks, coords))

    def accumulate(running_sum, entries):
        batch_values, batch_pots, block_list = entries
        tile_sum = jnp.einsum('pka,pjc->kjac', batch_values.astype(jnp.float32), batch_pots.astype(jnp.float32), precision=highest)
        return (running_sum.at[block_list[:, None], :, block_list[None, :], :].add(tile_sum), None)
    running_sum = jnp.zeros((BASIS_GROUP_NUM, BLK, BASIS_GROUP_NUM, BLK), jnp.float32)
    running_sum, unused = lax.scan(accumulate, running_sum, (sig_values, potentials, sig_blocks))
    exch_tile = running_sum.astype(jnp.bfloat16)
    strip_coeffs = jnp.transpose(lmo_coeffs.reshape(BASIS_GROUP_NUM, BLK, NSTRIP, LSTRIP), (2, 0, 1, 3))

    def one_strip(entries):
        coeff_strip, domain = entries
        exch_columns = exch_tile[:, :, domain, :].reshape(NAO, DOMN * BLK)
        coeff_rows = coeff_strip[domain].reshape(DOMN * BLK, LSTRIP)
        return lax.dot_general(coeff_rows, exch_columns, (((0,), (1,)), ((), ())), preferred_element_type=jnp.float32).astype(jnp.bfloat16)
    halves = lax.map(one_strip, (strip_coeffs, domain_blocks))
    return halves.reshape(NLMO, NAO)
```

```python
import functools
import math

import jax
import jax.numpy as jnp
from jax import lax
from jax.experimental import pallas as pl
from jax.experimental.pallas import tpu as pltpu
from jax.sharding import PartitionSpec as P

MESH = pl.DeviceIdType.MESH
VMEM_LIMIT = 60 * 1024 * 1024
f32 = jnp.float32
bf16 = jnp.bfloat16


def grid_split(grid_count):
    inner = max(1, math.isqrt(max(1, grid_count // 2)))
    while grid_count % inner:
        inner -= 1
    return grid_count // inner, inner


def tile_split(tile_count):
    inner = 2 if tile_count % 2 == 0 else 1
    return tile_count // inner, inner


def remote(src, dst, send_sem, recv_sem, device):
    return pltpu.make_async_remote_copy(
        src_ref=src,
        dst_ref=dst,
        send_sem=send_sem,
        recv_sem=recv_sem,
        device_id=device,
        device_id_type=MESH,
    )


def greet(devices):
    barrier = pltpu.get_barrier_semaphore()
    for device in devices:
        pl.semaphore_signal(barrier, inc=1, device_id=device, device_id_type=MESH)
    pl.semaphore_wait(barrier, len(devices))


def params(collective_id):
    return pltpu.CompilerParams(
        collective_id=collective_id, has_side_effects=True, vmem_limit_bytes=VMEM_LIMIT
    )


def vmem():
    return pl.BlockSpec(memory_space=pltpu.VMEM)


def spread_kernel(
    grid_count, tile_count, x_ref, all_ref, rows_ref, zs, zr, ys, yr, es, er, local_sem
):
    g, t = lax.axis_index("grid"), lax.axis_index("tile")
    nz, ny = grid_split(grid_count)
    z, y = g // ny, g % ny
    cols = x_ref.shape[1]
    rows = rows_ref.shape[2]
    offset = pl.multiple_of((g * rows) % cols, rows)
    owner = (g * rows) // cols == t

    z_peers = [(lax.rem(z + d, nz) * ny + y, t) for d in range(1, nz)]
    y_peers = [(z * ny + lax.rem(y + d, ny), t) for d in range(1, ny)]
    t_peers = [(g, lax.rem(t + d, tile_count)) for d in range(1, tile_count)]
    greet(z_peers + y_peers + t_peers)

    def z_source(dz):
        return lax.rem(z + nz - dz, nz)

    z_copies = [
        remote(x_ref, all_ref.at[g], zs.at[d], zr.at[d], z_peers[d]) for d in range(nz - 1)
    ]
    for copy in z_copies:
        copy.start()

    y_copies = {}

    def forward_y(dz):
        source = z_source(dz) * ny + y
        for d in range(ny - 1):
            block = x_ref if dz == 0 else all_ref.at[source]
            copy = remote(
                block, all_ref.at[source], ys.at[d, dz], yr.at[d, dz], y_peers[d]
            )
            copy.start()
            y_copies[d, dz] = copy

    def forward_rows(source, block):
        @pl.when(owner)
        def _():
            for d in range(tile_count - 1):
                remote(
                    block.at[:, pl.ds(offset, rows)],
                    rows_ref.at[source],
                    es.at[d],
                    er,
                    t_peers[d],
                ).start()

    forward_y(0)
    forward_rows(g, x_ref)
    keep = pltpu.make_async_copy(x_ref, all_ref.at[g], local_sem)
    keep.start()
    for dz in range(1, nz):
        source = z_source(dz) * ny + y
        z_copies[dz - 1].wait_recv()
        forward_y(dz)
        forward_rows(source, all_ref.at[source])
    for dz in range(nz):
        for d in range(ny - 1):
            source = z_source(dz) * ny + lax.rem(y + ny - d - 1, ny)
            y_copies[d, dz].wait_recv()
            forward_rows(source, all_ref.at[source])
    keep.wait()

    @pl.when(owner)
    def _():
        own = pltpu.make_async_copy(all_ref.at[:, :, pl.ds(offset, rows)], rows_ref, local_sem)
        own.start()
        for d in range(tile_count - 1):
            remote(rows_ref, rows_ref, es.at[d], er, t_peers[d]).wait_send()
        own.wait()

    @pl.when(jnp.logical_not(owner))
    def _():
        remote(rows_ref, rows_ref, es.at[0], er, t_peers[0]).wait_recv()

    for copy in z_copies:
        copy.wait_send()
    for copy in y_copies.values():
        copy.wait_send()


def spread(masked, grid_count, tile_count, rows):
    points, cols = masked.shape
    nz, ny = grid_split(grid_count)
    dma = pltpu.SemaphoreType.DMA
    return pl.pallas_call(
        functools.partial(spread_kernel, grid_count, tile_count),
        out_shape=(
            jax.ShapeDtypeStruct((grid_count, points, cols), bf16),
            jax.ShapeDtypeStruct((grid_count, points, rows), bf16),
        ),
        in_specs=[vmem()],
        out_specs=(vmem(), vmem()),
        scratch_shapes=[
            dma((nz,)),
            dma((nz,)),
            dma((ny, nz)),
            dma((ny, nz)),
            dma((tile_count,)),
            dma,
            dma,
        ],
        compiler_params=params(0),
    )(masked)


def reduce_kernel(
    grid_count,
    tile_count,
    part_ref,
    out_ref,
    sibling_ref,
    pair_ref,
    peer_ref,
    total_ref,
    cs,
    cr,
    xs,
    xr,
    gs,
    gr,
):
    g, t = lax.axis_index("grid"), lax.axis_index("tile")
    nx, nc = tile_split(tile_count)
    x, c = t // nc, t % nc
    sibling = 1 - c if nc == 2 else c
    x_peers = [(g, lax.rem(x + d, nx) * nc + c) for d in range(1, nx)]
    g_peers = [(lax.rem(g + d, grid_count), t) for d in range(1, grid_count)]
    c_peers = [(g, x * nc + sibling)] if nc == 2 else []
    greet(c_peers + x_peers + g_peers)

    c_copies = []
    if nc == 2:
        for d in range(nx):
            column = lax.rem(x + d, nx)
            c_copies.append(
                remote(
                    part_ref.at[:, column, sibling],
                    sibling_ref.at[:, column],
                    cs.at[d],
                    cr.at[d],
                    c_peers[0],
                )
            )
        order = list(range(1, nx)) + [0]
        for d in order:
            c_copies[d].start()

    def pair(d):
        column = lax.rem(x + d, nx)
        if nc == 2:
            c_copies[d].wait_recv()

        @pl.loop(0, grid_count)
        def _(i):
            value = part_ref[i, column, c].astype(f32)
            if nc == 2:
                value = value + sibling_ref[i, column].astype(f32)
            pair_ref[d, i] = value.astype(bf16)

    x_copies = []
    for d in range(1, nx):
        pair(d)
        copy = remote(
            pair_ref.at[d], peer_ref.at[d], xs.at[d], xr.at[d], x_peers[d - 1]
        )
        copy.start()
        x_copies.append(copy)
    pair(0)
    for copy in x_copies:
        copy.wait_recv()

    @pl.loop(0, grid_count)
    def _(i):
        value = pair_ref[0, i].astype(f32)
        for d in range(1, nx):
            value = value + peer_ref[d, i].astype(f32)
        total_ref[i] = value.astype(bf16)

    g_copies = []
    for d in range(1, grid_count):
        target = lax.rem(g + d, grid_count)
        copy = remote(
            total_ref.at[target], out_ref.at[g], gs.at[d], gr.at[d], g_peers[d - 1]
        )
        copy.start()
        g_copies.append(copy)
    out_ref[g] = total_ref[g]
    for copy in c_copies:
        copy.wait_send()
    for copy in x_copies:
        copy.wait_send()
    for copy in g_copies:
        copy.wait()


def reduce_parts(parts, grid_count, tile_count):
    nx, nc = tile_split(tile_count)
    points, rows = parts.shape
    slab = points // (grid_count * tile_count)
    dma = pltpu.SemaphoreType.DMA
    return pl.pallas_call(
        functools.partial(reduce_kernel, grid_count, tile_count),
        out_shape=jax.ShapeDtypeStruct((grid_count, slab, rows), bf16),
        in_specs=[vmem()],
        out_specs=vmem(),
        scratch_shapes=[
            pltpu.VMEM((grid_count, nx, slab, rows), bf16),
            pltpu.VMEM((nx, grid_count, slab, rows), bf16),
            pltpu.VMEM((nx, grid_count, slab, rows), bf16),
            pltpu.VMEM((grid_count, slab, rows), bf16),
            dma((nx,)),
            dma((nx,)),
            dma((nx,)),
            dma((nx,)),
            dma((grid_count,)),
            dma((grid_count,)),
        ],
        compiler_params=params(1),
    )(parts.reshape(grid_count, nx, nc, slab, rows))


def finish_kernel(
    grid_count,
    tile_count,
    pot_ref,
    lmo_hbm,
    mask_ref,
    rows_ref,
    out_ref,
    lmo_ref,
    got_ref,
    flat_ref,
    send_ref,
    part_ref,
    own_ref,
    all_ref,
    lmo_sem,
    vs,
    vr,
    ws,
    wr,
    gs,
    gr,
):
    g, t = lax.axis_index("grid"), lax.axis_index("tile")
    load = pltpu.make_async_copy(lmo_hbm, lmo_ref, lmo_sem)
    load.start()
    t_peers = [(g, lax.rem(t + d, tile_count)) for d in range(1, tile_count)]
    g_peers = [(lax.rem(g + d, grid_count), t) for d in range(1, grid_count)]
    greet(t_peers + g_peers)
    cols = mask_ref.shape[0]
    slab = pot_ref.shape[1]
    block = pot_ref.shape[2]
    strip = own_ref.shape[1]

    v_copies = []
    for d in range(1, tile_count):
        target = lax.rem(t + d, tile_count)
        copy = remote(
            pot_ref.at[pl.ds(target * cols, cols)],
            got_ref.at[t],
            vs.at[d],
            vr.at[d],
            t_peers[d - 1],
        )
        copy.start()
        v_copies.append(copy)
    got_ref[t] = pot_ref[pl.ds(t * cols, cols)]
    for copy in v_copies:
        copy.wait()
    for i in range(tile_count):
        for m in range(cols):
            flat_ref[m, i * slab : (i + 1) * slab, :] = got_ref[i, m].astype(f32)
    load.wait()
    for s in range(tile_count):
        lanes = slice(s * strip, (s + 1) * strip)
        total = None
        for m in range(cols):
            term = mask_ref[m : m + 1, lanes] * jnp.dot(
                flat_ref[m].astype(bf16),
                lmo_ref[m * block : (m + 1) * block, lanes],
                preferred_element_type=f32,
            )
            total = term if total is None else total + term
        send_ref[s] = total.astype(bf16)
    w_copies = []
    for d in range(1, tile_count):
        target = lax.rem(t + d, tile_count)
        copy = remote(
            send_ref.at[target], part_ref.at[d], ws.at[d], wr.at[d], t_peers[d - 1]
        )
        copy.start()
        w_copies.append(copy)
    total = send_ref[t].astype(f32)
    for d, copy in enumerate(w_copies):
        copy.wait()
        total = total + part_ref[d + 1].astype(f32)
    own_ref[...] = total.astype(bf16)
    g_copies = []
    for d in range(1, grid_count):
        copy = remote(own_ref, all_ref.at[g], gs.at[d], gr.at[d], g_peers[d - 1])
        copy.start()
        g_copies.append(copy)
    all_ref[g] = own_ref[...]
    for copy in g_copies:
        copy.wait()
    points = grid_count * own_ref.shape[0]
    weights = all_ref[...].astype(f32).reshape(points, strip).T.astype(bf16)
    rows = out_ref.shape[1]
    step = min(rows, 512)
    for i in range(rows // step):
        lanes = slice(i * step, (i + 1) * step)
        out_ref[:, lanes] = jnp.dot(
            weights,
            rows_ref[:, :, lanes].reshape(points, step),
            preferred_element_type=f32,
        ).astype(bf16)


def finish(potential, lmo_coeffs, mask, rows, grid_count, tile_count):
    blocks, slab, block = potential.shape
    cols = blocks // tile_count
    total = lmo_coeffs.shape[1]
    strip = total // tile_count
    batch = rows.shape[1]
    dma = pltpu.SemaphoreType.DMA
    return pl.pallas_call(
        functools.partial(finish_kernel, grid_count, tile_count),
        out_shape=jax.ShapeDtypeStruct((strip, rows.shape[2]), bf16),
        in_specs=[vmem(), pl.BlockSpec(memory_space=pl.ANY), vmem(), vmem()],
        out_specs=vmem(),
        scratch_shapes=[
            pltpu.VMEM(lmo_coeffs.shape, bf16),
            pltpu.VMEM((tile_count, cols, slab, block), bf16),
            pltpu.VMEM((cols, batch, block), f32),
            pltpu.VMEM((tile_count, batch, strip), bf16),
            pltpu.VMEM((tile_count, batch, strip), bf16),
            pltpu.VMEM((batch, strip), bf16),
            pltpu.VMEM((grid_count, batch, strip), bf16),
            dma,
            dma((tile_count,)),
            dma((tile_count,)),
            dma((tile_count,)),
            dma((tile_count,)),
            dma((grid_count,)),
            dma((grid_count,)),
        ],
        compiler_params=params(2),
    )(potential, lmo_coeffs, mask, rows)


def shards(
    point_values,
    sig_blocks,
    density,
    coulomb_core,
    screen_mask,
    ao_centers,
    ao_widths,
    point_coords,
    lmo_coeffs,
    domain_blocks,
):
    grid_count = lax.axis_size("grid")
    tile_count = lax.axis_size("tile")
    panel = lax.axis_index("tile")
    own_rows, own_cols = density.shape
    points = point_values.shape[0]
    block_size = coulomb_core.shape[0]
    total_aos = ao_widths.shape[0]
    all_blocks = total_aos // block_size
    col_blocks = own_cols // block_size
    slab = points // tile_count
    block_ids = jnp.arange(all_blocks, dtype=jnp.int32)
    named = jnp.any(sig_blocks[0][:, None] == block_ids[None, :], axis=0)
    first_col = panel * col_blocks
    named_cols = lax.dynamic_slice_in_dim(named.astype(f32), first_col, col_blocks, 0)
    col_mask = jnp.repeat(named_cols, block_size)
    masked = point_values * col_mask[None, :].astype(bf16)
    all_values, row_values = spread(masked, grid_count, tile_count, own_rows)
    parts = lax.dot_general(
        all_values.reshape(grid_count * points, own_cols),
        density,
        (((1,), (1,)), ((), ())),
        preferred_element_type=f32,
    ).astype(bf16)
    summed = reduce_parts(parts, grid_count, tile_count)
    row_blocks = own_rows // block_size
    term = summed.astype(f32).reshape(grid_count, slab, row_blocks, block_size)
    term = jnp.transpose(term, (0, 2, 1, 3)).reshape(all_blocks, slab, block_size)
    coords = lax.dynamic_slice_in_dim(point_coords, panel * slab, slab, 1)
    offsets = (
        ao_centers.reshape(3, all_blocks, 1, block_size) - coords.reshape(3, 1, slab, 1)
    )
    coefficient = 1.0 / jnp.sqrt(
        jnp.sum(offsets * offsets, axis=0) + ao_widths.reshape(all_blocks, 1, block_size)
    )
    scaled = coefficient * named.astype(f32)[:, None, None]
    weighted = (scaled * term).astype(bf16)
    screened = jnp.einsum(
        "kj,jpa->kpa", screen_mask.astype(bf16), weighted, preferred_element_type=f32
    ).astype(bf16)
    mixed = jnp.einsum(
        "kpc,ac->kpa", screened, coulomb_core, preferred_element_type=f32
    )
    potential = (scaled * mixed).astype(bf16)
    local_ids = first_col + jnp.arange(col_blocks, dtype=jnp.int32)
    in_domain = jnp.any(domain_blocks[:, :, None] == local_ids[None, None, :], axis=1)
    strip_width = lmo_coeffs.shape[1] // domain_blocks.shape[0]
    mask = jnp.repeat(jnp.transpose(in_domain).astype(f32), strip_width, axis=1)
    return finish(potential, lmo_coeffs, mask, row_values, grid_count, tile_count)


def solution(mesh):
    in_specs = (
        P("grid", "tile"),
        P("grid", None),
        P("grid", "tile"),
        P(),
        P(),
        P(),
        P(),
        P(None, "grid"),
        P("tile", None),
        P(),
    )
    out_specs = P("tile", "grid")
    return jax.shard_map(shards, mesh=mesh, in_specs=in_specs, out_specs=out_specs, check_vma=False)
```

```python
import functools
import math

import jax
import jax.numpy as jnp
from jax import lax
from jax.experimental import pallas as pl
from jax.experimental.pallas import tpu as pltpu
from jax.sharding import PartitionSpec as P

MESH = pl.DeviceIdType.MESH
VMEM_LIMIT = 60 * 1024 * 1024
f32 = jnp.float32
bf16 = jnp.bfloat16


def grid_split(grid_count):
    inner = max(1, math.isqrt(max(1, grid_count // 2)))
    while grid_count % inner:
        inner -= 1
    return grid_count // inner, inner


def tile_split(tile_count):
    inner = 2 if tile_count % 2 == 0 else 1
    return tile_count // inner, inner


def remote(src, dst, send_sem, recv_sem, device):
    return pltpu.make_async_remote_copy(
        src_ref=src,
        dst_ref=dst,
        send_sem=send_sem,
        recv_sem=recv_sem,
        device_id=device,
        device_id_type=MESH,
    )


def greet(devices):
    barrier = pltpu.get_barrier_semaphore()
    for device in devices:
        pl.semaphore_signal(barrier, inc=1, device_id=device, device_id_type=MESH)
    pl.semaphore_wait(barrier, len(devices))


def params(collective_id):
    return pltpu.CompilerParams(
        collective_id=collective_id, has_side_effects=True, vmem_limit_bytes=VMEM_LIMIT
    )


def vmem():
    return pl.BlockSpec(memory_space=pltpu.VMEM)


def spread_kernel(
    grid_count, tile_count, x_ref, all_ref, rows_ref, zs, zr, ys, yr, es, er, local_sem
):
    g, t = lax.axis_index("grid"), lax.axis_index("tile")
    nz, ny = grid_split(grid_count)
    nx, nc = tile_split(tile_count)
    z, y = g // ny, g % ny
    x, c = t // nc, t % nc
    cols = x_ref.shape[1]
    rows = rows_ref.shape[2]
    offset = pl.multiple_of((g * rows) % cols, rows)
    owner = (g * rows) // cols
    is_owner = owner == t
    in_column = owner % nc == c
    has_left, has_right = z > 0, z < nz - 1
    left = (lax.rem(z + nz - 1, nz) * ny + y, t)
    right = (lax.rem(z + 1, nz) * ny + y, t)
    y_peers = [(z * ny + lax.rem(y + d, ny), t) for d in range(1, ny)]
    x_peers = [(g, lax.rem(x + d, nx) * nc + c) for d in range(1, nx)]
    c_peers = [(g, x * nc + (1 - c))] if nc == 2 else []
    greet([left, right] + y_peers + x_peers + c_peers)

    def present(k):
        if k == 0:
            return z >= 0
        step = (k + 1) // 2
        return z >= step if k % 2 else z <= nz - 1 - step

    def source(k, d):
        step = (k + 1) // 2
        line = lax.rem(z + nz - step, nz) if k % 2 else lax.rem(z + step, nz)
        return line * ny + lax.rem(y + ny - d, ny)

    def block(k, d):
        return x_ref if k == 0 and d == 0 else all_ref.at[source(k, d)]

    def along(k, to_right):
        step = (k + 1) // 2
        lane = 0 if to_right else 1
        return remote(
            block(k, 0),
            all_ref.at[source(k, 0)],
            zs.at[lane, step],
            zr.at[lane, step],
            right if to_right else left,
        )

    def across(k, d):
        return remote(
            block(k, 0), all_ref.at[source(k, 0)], ys.at[d, k], yr.at[d, k], y_peers[d - 1]
        )

    def arrived(k, d, sends, recvs):
        spot = all_ref.at[source(k, d)]
        remote(spot, spot, sends, recvs, right).wait_recv()

    def share(k, d):
        for i, peer in enumerate(x_peers + c_peers):
            remote(
                block(k, d).at[:, pl.ds(offset, rows)],
                rows_ref.at[source(k, d)],
                es.at[i],
                er.at[d, k],
                peer,
            ).start()

    steps = range(2 * nz - 1)

    def send_block(k):
        if k == 0 or k % 2:

            @pl.when(has_right)
            def _():
                along(k, True).start()

        if k == 0 or k % 2 == 0:

            @pl.when(has_left)
            def _():
                along(k, False).start()

        for d in range(1, ny):
            across(k, d).start()

        @pl.when(is_owner)
        def _():
            share(k, 0)

    def take_across(k):
        @pl.when(present(k))
        def _():
            for d in range(1, ny):
                arrived(k, d, ys.at[d, k], yr.at[d, k])

                @pl.when(is_owner)
                def _():
                    share(k, d)

    send_block(0)
    keep = pltpu.make_async_copy(x_ref, all_ref.at[g], local_sem)
    keep.start()
    for step in range(1, nz):
        for k in (2 * step - 1, 2 * step):

            @pl.when(present(k))
            def _():
                lane = 0 if k % 2 else 1
                arrived(k, 0, zs.at[lane, step - 1], zr.at[lane, step - 1])
                send_block(k)

        if step == 1:
            take_across(0)
        else:
            take_across(2 * step - 3)
            take_across(2 * step - 2)
    if nz > 1:
        take_across(2 * nz - 3)
        take_across(2 * nz - 2)
    else:
        take_across(0)
    keep.wait()

    @pl.when(is_owner)
    def _():
        own = pltpu.make_async_copy(all_ref.at[:, :, pl.ds(offset, rows)], rows_ref, local_sem)
        own.start()
        for i in range(len(x_peers + c_peers)):
            remote(rows_ref, rows_ref, es.at[i], er.at[0, 0], right).wait_send()
        own.wait()

    @pl.when(jnp.logical_not(is_owner))
    def _():
        for k in steps:

            @pl.when(present(k))
            def _():
                for d in range(ny):
                    spot = rows_ref.at[source(k, d)]
                    pass_on = remote(
                        spot, spot, es.at[nx - 1], er.at[d, k], (c_peers or [right])[0]
                    )
                    pass_on.wait_recv()
                    if nc == 2:

                        @pl.when(in_column)
                        def _():
                            pass_on.start()

        if nc == 2:

            @pl.when(in_column)
            def _():
                remote(rows_ref, rows_ref, es.at[nx - 1], er.at[0, 0], right).wait_send()

    for k in steps:

        @pl.when(present(k))
        def _():
            if k == 0 or k % 2:

                @pl.when(has_right)
                def _():
                    along(k, True).wait_send()

            if k == 0 or k % 2 == 0:

                @pl.when(has_left)
                def _():
                    along(k, False).wait_send()

            for d in range(1, ny):
                across(k, d).wait_send()


def spread(masked, grid_count, tile_count, rows):
    points, cols = masked.shape
    nz, ny = grid_split(grid_count)
    nx, nc = tile_split(tile_count)
    dma = pltpu.SemaphoreType.DMA
    return pl.pallas_call(
        functools.partial(spread_kernel, grid_count, tile_count),
        out_shape=(
            jax.ShapeDtypeStruct((grid_count, points, cols), bf16),
            jax.ShapeDtypeStruct((grid_count, points, rows), bf16),
        ),
        in_specs=[vmem()],
        out_specs=(vmem(), vmem()),
        scratch_shapes=[
            dma((2, nz)),
            dma((2, nz)),
            dma((ny, 2 * nz)),
            dma((ny, 2 * nz)),
            dma((nx,)),
            dma((ny, 2 * nz)),
            dma,
        ],
        compiler_params=params(0),
    )(masked)


def reduce_kernel(
    grid_count,
    tile_count,
    part_ref,
    out_ref,
    sibling_ref,
    pair_ref,
    peer_ref,
    total_ref,
    cs,
    cr,
    xs,
    xr,
    gs,
    gr,
):
    g, t = lax.axis_index("grid"), lax.axis_index("tile")
    nx, nc = tile_split(tile_count)
    x, c = t // nc, t % nc
    sibling = 1 - c if nc == 2 else c
    x_peers = [(g, lax.rem(x + d, nx) * nc + c) for d in range(1, nx)]
    g_peers = [(lax.rem(g + d, grid_count), t) for d in range(1, grid_count)]
    c_peers = [(g, x * nc + sibling)] if nc == 2 else []
    greet(c_peers + x_peers + g_peers)

    c_copies = []
    if nc == 2:
        for d in range(nx):
            column = lax.rem(x + d, nx)
            c_copies.append(
                remote(
                    part_ref.at[:, column, sibling],
                    sibling_ref.at[:, column],
                    cs.at[d],
                    cr.at[d],
                    c_peers[0],
                )
            )
        order = list(range(1, nx)) + [0]
        for d in order:
            c_copies[d].start()

    def pair(d):
        column = lax.rem(x + d, nx)
        if nc == 2:
            c_copies[d].wait_recv()

        @pl.loop(0, grid_count)
        def _(i):
            value = part_ref[i, column, c].astype(f32)
            if nc == 2:
                value = value + sibling_ref[i, column].astype(f32)
            pair_ref[d, i] = value.astype(bf16)

    x_copies = []
    for d in range(1, nx):
        pair(d)
        copy = remote(
            pair_ref.at[d], peer_ref.at[d], xs.at[d], xr.at[d], x_peers[d - 1]
        )
        copy.start()
        x_copies.append(copy)
    pair(0)
    for copy in x_copies:
        copy.wait_recv()

    @pl.loop(0, grid_count)
    def _(i):
        value = pair_ref[0, i].astype(f32)
        for d in range(1, nx):
            value = value + peer_ref[d, i].astype(f32)
        total_ref[i] = value.astype(bf16)

    g_copies = []
    for d in range(1, grid_count):
        target = lax.rem(g + d, grid_count)
        copy = remote(
            total_ref.at[target], out_ref.at[g], gs.at[d], gr.at[d], g_peers[d - 1]
        )
        copy.start()
        g_copies.append(copy)
    out_ref[g] = total_ref[g]
    for copy in c_copies:
        copy.wait_send()
    for copy in x_copies:
        copy.wait_send()
    for copy in g_copies:
        copy.wait()


def reduce_parts(parts, grid_count, tile_count):
    nx, nc = tile_split(tile_count)
    points, rows = parts.shape
    slab = points // (grid_count * tile_count)
    dma = pltpu.SemaphoreType.DMA
    return pl.pallas_call(
        functools.partial(reduce_kernel, grid_count, tile_count),
        out_shape=jax.ShapeDtypeStruct((grid_count, slab, rows), bf16),
        in_specs=[vmem()],
        out_specs=vmem(),
        scratch_shapes=[
            pltpu.VMEM((grid_count, nx, slab, rows), bf16),
            pltpu.VMEM((nx, grid_count, slab, rows), bf16),
            pltpu.VMEM((nx, grid_count, slab, rows), bf16),
            pltpu.VMEM((grid_count, slab, rows), bf16),
            dma((nx,)),
            dma((nx,)),
            dma((nx,)),
            dma((nx,)),
            dma((grid_count,)),
            dma((grid_count,)),
        ],
        compiler_params=params(1),
    )(parts.reshape(grid_count, nx, nc, slab, rows))


def finish_kernel(
    grid_count,
    tile_count,
    pot_ref,
    lmo_hbm,
    mask_ref,
    all_ref,
    lmo_ref,
    got_ref,
    flat_ref,
    send_ref,
    part_ref,
    own_ref,
    lmo_sem,
    vs,
    vr,
    ws,
    wr,
    gs,
    gr,
):
    g, t = lax.axis_index("grid"), lax.axis_index("tile")
    load = pltpu.make_async_copy(lmo_hbm, lmo_ref, lmo_sem)
    load.start()
    t_peers = [(g, lax.rem(t + d, tile_count)) for d in range(1, tile_count)]
    g_peers = [(lax.rem(g + d, grid_count), t) for d in range(1, grid_count)]
    greet(t_peers + g_peers)
    cols = mask_ref.shape[0]
    slab = pot_ref.shape[1]
    block = pot_ref.shape[2]
    strip = own_ref.shape[1]

    v_copies = []
    for d in range(1, tile_count):
        target = lax.rem(t + d, tile_count)
        copy = remote(
            pot_ref.at[pl.ds(target * cols, cols)],
            got_ref.at[t],
            vs.at[d],
            vr.at[d],
            t_peers[d - 1],
        )
        copy.start()
        v_copies.append(copy)
    got_ref[t] = pot_ref[pl.ds(t * cols, cols)]
    for copy in v_copies:
        copy.wait()
    for i in range(tile_count):
        for m in range(cols):
            flat_ref[m, i * slab : (i + 1) * slab, :] = got_ref[i, m].astype(f32)
    load.wait()
    for s in range(tile_count):
        lanes = slice(s * strip, (s + 1) * strip)
        total = None
        for m in range(cols):
            term = mask_ref[m : m + 1, lanes] * jnp.dot(
                flat_ref[m].astype(bf16),
                lmo_ref[m * block : (m + 1) * block, lanes],
                preferred_element_type=f32,
            )
            total = term if total is None else total + term
        send_ref[s] = total.astype(bf16)
    w_copies = []
    for d in range(1, tile_count):
        target = lax.rem(t + d, tile_count)
        copy = remote(
            send_ref.at[target], part_ref.at[d], ws.at[d], wr.at[d], t_peers[d - 1]
        )
        copy.start()
        w_copies.append(copy)
    total = send_ref[t].astype(f32)
    for d, copy in enumerate(w_copies):
        copy.wait()
        total = total + part_ref[d + 1].astype(f32)
    own_ref[...] = total.astype(bf16)
    g_copies = []
    for d in range(1, grid_count):
        copy = remote(own_ref, all_ref.at[g], gs.at[d], gr.at[d], g_peers[d - 1])
        copy.start()
        g_copies.append(copy)
    all_ref[g] = own_ref[...]
    for copy in g_copies:
        copy.wait()


def finish(potential, lmo_coeffs, mask, batch, grid_count, tile_count):
    blocks, slab, block = potential.shape
    cols = blocks // tile_count
    total = lmo_coeffs.shape[1]
    strip = total // tile_count
    dma = pltpu.SemaphoreType.DMA
    return pl.pallas_call(
        functools.partial(finish_kernel, grid_count, tile_count),
        out_shape=jax.ShapeDtypeStruct((grid_count, batch, strip), bf16),
        in_specs=[vmem(), pl.BlockSpec(memory_space=pl.ANY), vmem()],
        out_specs=vmem(),
        scratch_shapes=[
            pltpu.VMEM(lmo_coeffs.shape, bf16),
            pltpu.VMEM((tile_count, cols, slab, block), bf16),
            pltpu.VMEM((cols, batch, block), f32),
            pltpu.VMEM((tile_count, batch, strip), bf16),
            pltpu.VMEM((tile_count, batch, strip), bf16),
            pltpu.VMEM((batch, strip), bf16),
            dma,
            dma((tile_count,)),
            dma((tile_count,)),
            dma((tile_count,)),
            dma((tile_count,)),
            dma((grid_count,)),
            dma((grid_count,)),
        ],
        compiler_params=params(2),
    )(potential, lmo_coeffs, mask)


def shards(
    point_values,
    sig_blocks,
    density,
    coulomb_core,
    screen_mask,
    ao_centers,
    ao_widths,
    point_coords,
    lmo_coeffs,
    domain_blocks,
):
    grid_count = lax.axis_size("grid")
    tile_count = lax.axis_size("tile")
    panel = lax.axis_index("tile")
    own_rows, own_cols = density.shape
    points = point_values.shape[0]
    block_size = coulomb_core.shape[0]
    total_aos = ao_widths.shape[0]
    all_blocks = total_aos // block_size
    col_blocks = own_cols // block_size
    slab = points // tile_count
    block_ids = jnp.arange(all_blocks, dtype=jnp.int32)
    named = jnp.any(sig_blocks[0][:, None] == block_ids[None, :], axis=0)
    first_col = panel * col_blocks
    named_cols = lax.dynamic_slice_in_dim(named.astype(f32), first_col, col_blocks, 0)
    col_mask = jnp.repeat(named_cols, block_size)
    masked = point_values * col_mask[None, :].astype(bf16)
    all_values, row_values = spread(masked, grid_count, tile_count, own_rows)
    parts = lax.dot_general(
        all_values.reshape(grid_count * points, own_cols),
        density,
        (((1,), (1,)), ((), ())),
        preferred_element_type=f32,
    ).astype(bf16)
    summed = reduce_parts(parts, grid_count, tile_count)
    row_blocks = own_rows // block_size
    term = summed.astype(f32).reshape(grid_count, slab, row_blocks, block_size)
    term = jnp.transpose(term, (0, 2, 1, 3)).reshape(all_blocks, slab, block_size)
    coords = lax.dynamic_slice_in_dim(point_coords, panel * slab, slab, 1)
    offsets = (
        ao_centers.reshape(3, all_blocks, 1, block_size) - coords.reshape(3, 1, slab, 1)
    )
    coefficient = 1.0 / jnp.sqrt(
        jnp.sum(offsets * offsets, axis=0) + ao_widths.reshape(all_blocks, 1, block_size)
    )
    scaled = coefficient * named.astype(f32)[:, None, None]
    weighted = (scaled * term).astype(bf16)
    screened = jnp.einsum(
        "kj,jpa->kpa", screen_mask.astype(bf16), weighted, preferred_element_type=f32
    ).astype(bf16)
    mixed = jnp.einsum(
        "kpc,ac->kpa", screened, coulomb_core, preferred_element_type=f32
    )
    potential = (scaled * mixed).astype(bf16)
    local_ids = first_col + jnp.arange(col_blocks, dtype=jnp.int32)
    in_domain = jnp.any(domain_blocks[:, :, None] == local_ids[None, None, :], axis=1)
    strip_width = lmo_coeffs.shape[1] // domain_blocks.shape[0]
    mask = jnp.repeat(jnp.transpose(in_domain).astype(f32), strip_width, axis=1)
    weights = finish(potential, lmo_coeffs, mask, points, grid_count, tile_count)
    return lax.dot_general(
        weights.reshape(grid_count * points, weights.shape[2]),
        row_values.reshape(grid_count * points, own_rows),
        (((0,), (0,)), ((), ())),
        preferred_element_type=f32,
    ).astype(bf16)


def solution(mesh):
    in_specs = (
        P("grid", "tile"),
        P("grid", None),
        P("grid", "tile"),
        P(),
        P(),
        P(),
        P(),
        P(None, "grid"),
        P("tile", None),
        P(),
    )
    out_specs = P("tile", "grid")
    return jax.shard_map(shards, mesh=mesh, in_specs=in_specs, out_specs=out_specs, check_vma=False)
```

```python
import functools
import math

import jax
import jax.numpy as jnp
from jax import lax
from jax.experimental import pallas as pl
from jax.experimental.pallas import tpu as pltpu
from jax.sharding import PartitionSpec as P

MESH = pl.DeviceIdType.MESH
VMEM_LIMIT = 60 * 1024 * 1024
f32 = jnp.float32
bf16 = jnp.bfloat16


def grid_split(grid_count):
    inner = max(1, math.isqrt(max(1, grid_count // 2)))
    while grid_count % inner:
        inner -= 1
    return grid_count // inner, inner


def tile_split(tile_count):
    inner = 2 if tile_count % 2 == 0 else 1
    return tile_count // inner, inner


def remote(src, dst, send_sem, recv_sem, device):
    return pltpu.make_async_remote_copy(
        src_ref=src,
        dst_ref=dst,
        send_sem=send_sem,
        recv_sem=recv_sem,
        device_id=device,
        device_id_type=MESH,
    )


def greet(devices):
    barrier = pltpu.get_barrier_semaphore()
    for device in devices:
        pl.semaphore_signal(barrier, inc=1, device_id=device, device_id_type=MESH)
    pl.semaphore_wait(barrier, len(devices))


def params(collective_id):
    return pltpu.CompilerParams(
        collective_id=collective_id, has_side_effects=True, vmem_limit_bytes=VMEM_LIMIT
    )


def vmem():
    return pl.BlockSpec(memory_space=pltpu.VMEM)


def front_kernel(
    grid_count,
    tile_count,
    x_ref,
    density_hbm,
    out_ref,
    rows_ref,
    all_ref,
    density_ref,
    part_ref,
    sibling_ref,
    pair_ref,
    peer_ref,
    total_ref,
    zs,
    zr,
    ys,
    yr,
    es,
    er,
    local_sem,
    ds,
    cs,
    cr,
    xs,
    xr,
    gs,
    gr,
):
    chunks, slab, width = part_ref.shape[0], part_ref.shape[4], part_ref.shape[5]
    loads = [
        pltpu.make_async_copy(
            density_hbm.at[pl.ds(i * width, width)],
            density_ref.at[pl.ds(i * width, width)],
            ds.at[i],
        )
        for i in range(chunks)
    ]
    g, t = lax.axis_index("grid"), lax.axis_index("tile")
    nz, ny = grid_split(grid_count)
    nx, nc = tile_split(tile_count)
    z, y = g // ny, g % ny
    x, c = t // nc, t % nc
    cols = x_ref.shape[1]
    rows = rows_ref.shape[2]
    offset = pl.multiple_of((g * rows) % cols, rows)
    owner = (g * rows) // cols
    is_owner = owner == t
    in_column = owner % nc == c
    has_left, has_right = z > 0, z < nz - 1
    left = (lax.rem(z + nz - 1, nz) * ny + y, t)
    right = (lax.rem(z + 1, nz) * ny + y, t)
    y_peers = [(z * ny + lax.rem(y + d, ny), t) for d in range(1, ny)]
    x_peers = [(g, lax.rem(x + d, nx) * nc + c) for d in range(1, nx)]
    c_peers = [(g, x * nc + (1 - c))] if nc == 2 else []
    g_peers = [(lax.rem(g + d, grid_count), t) for d in range(1, grid_count)]
    greet(g_peers + x_peers + c_peers)

    def present(k):
        if k == 0:
            return z >= 0
        step = (k + 1) // 2
        return z >= step if k % 2 else z <= nz - 1 - step

    def source(k, d):
        step = (k + 1) // 2
        line = lax.rem(z + nz - step, nz) if k % 2 else lax.rem(z + step, nz)
        return line * ny + lax.rem(y + ny - d, ny)

    def block(k, d):
        return x_ref if k == 0 and d == 0 else all_ref.at[source(k, d)]

    def along(k, to_right):
        step = (k + 1) // 2
        lane = 0 if to_right else 1
        return remote(
            block(k, 0),
            all_ref.at[source(k, 0)],
            zs.at[lane, step],
            zr.at[lane, step],
            right if to_right else left,
        )

    def across(k, d):
        return remote(
            block(k, 0), all_ref.at[source(k, 0)], ys.at[d, k], yr.at[d, k], y_peers[d - 1]
        )

    def arrived(k, d, sends, recvs):
        spot = all_ref.at[source(k, d)]
        remote(spot, spot, sends, recvs, right).wait_recv()

    def share(k, d):
        for i, peer in enumerate(x_peers + c_peers):
            remote(
                block(k, d).at[:, pl.ds(offset, rows)],
                rows_ref.at[source(k, d)],
                es.at[i],
                er.at[d, k],
                peer,
            ).start()

    steps = range(2 * nz - 1)

    def send_block(k):
        if k == 0 or k % 2:

            @pl.when(has_right)
            def _():
                along(k, True).start()

        if k == 0 or k % 2 == 0:

            @pl.when(has_left)
            def _():
                along(k, False).start()

        for d in range(1, ny):
            across(k, d).start()

        @pl.when(is_owner)
        def _():
            share(k, 0)

    def take_across(k):
        @pl.when(present(k))
        def _():
            for d in range(1, ny):
                arrived(k, d, ys.at[d, k], yr.at[d, k])

                @pl.when(is_owner)
                def _():
                    share(k, d)

    send_block(0)
    keep = pltpu.make_async_copy(x_ref, all_ref.at[g], local_sem)
    keep.start()
    for load in loads:
        load.start()
    for step in range(1, nz):
        for k in (2 * step - 1, 2 * step):

            @pl.when(present(k))
            def _():
                lane = 0 if k % 2 else 1
                arrived(k, 0, zs.at[lane, step - 1], zr.at[lane, step - 1])
                send_block(k)

        if step == 1:
            take_across(0)
        else:
            take_across(2 * step - 3)
            take_across(2 * step - 2)
    if nz > 1:
        take_across(2 * nz - 3)
        take_across(2 * nz - 2)
    else:
        take_across(0)
    keep.wait()
    batch = x_ref.shape[0]
    points = grid_count * batch
    order = list(range(1, nx)) + [0]

    def product(i):
        loads[i].wait()
        value = lax.dot_general(
            all_ref[...].reshape(points, cols),
            density_ref[i * width : (i + 1) * width, :],
            (((1,), (1,)), ((), ())),
            preferred_element_type=f32,
        )
        if slab % 8 == 0:
            part_ref[i] = value.reshape(grid_count, nx, nc, slab, width).astype(bf16)
        else:
            for n in range(points // slab):
                part_ref[i, n // (nx * nc), n // nc % nx, n % nc] = value[
                    n * slab : (n + 1) * slab
                ].astype(bf16)

    def core_copy(i, d):
        column = lax.rem(x + d, nx)
        return remote(
            part_ref.at[i, :, column, 1 - c],
            sibling_ref.at[i, :, column],
            cs.at[i, d],
            cr.at[i, d],
            c_peers[0],
        )

    def pair_copy(i, d):
        return remote(
            pair_ref.at[i, d], peer_ref.at[i, d], xs.at[i, d], xr.at[i, d], x_peers[d - 1]
        )

    def exchange(i):
        for d in order:
            column = lax.rem(x + d, nx)
            if nc == 2:
                core_copy(i, d).wait_recv()

            @pl.loop(0, grid_count)
            def _(n):
                value = part_ref[i, n, column, c].astype(f32)
                if nc == 2:
                    value = value + sibling_ref[i, n, column].astype(f32)
                pair_ref[i, d, n] = value.astype(bf16)

            if d:
                pair_copy(i, d).start()

    def pass_rows():
        @pl.when(jnp.logical_not(is_owner))
        def _():
            for k in steps:

                @pl.when(present(k))
                def _():
                    for d in range(ny):
                        spot = rows_ref.at[source(k, d)]
                        pass_on = remote(
                            spot, spot, es.at[nx - 1], er.at[d, k], (c_peers or [right])[0]
                        )
                        if nc == 2:

                            @pl.when(in_column)
                            def _():
                                pass_on.wait_recv()
                                pass_on.start()

    own = pltpu.make_async_copy(all_ref.at[:, :, pl.ds(offset, rows)], rows_ref, local_sem)

    @pl.when(is_owner)
    def _():
        own.start()

    for i in range(chunks):
        product(i)
        if nc == 2:
            for d in order:
                core_copy(i, d).start()
        if i == 0:
            pass_rows()
        else:
            exchange(i - 1)
    exchange(chunks - 1)

    for i in range(chunks):
        for d in range(1, nx):
            pair_copy(i, d).wait_recv()

        @pl.loop(0, grid_count)
        def _(n):
            value = pair_ref[i, 0, n].astype(f32)
            for d in range(1, nx):
                value = value + peer_ref[i, d, n].astype(f32)
            total_ref[n, :, i * width : (i + 1) * width] = value.astype(bf16)

    g_copies = []
    for d in range(1, grid_count):
        target = lax.rem(g + d, grid_count)
        copy = remote(
            total_ref.at[target], out_ref.at[g], gs.at[d], gr.at[d], g_peers[d - 1]
        )
        copy.start()
        g_copies.append(copy)
    out_ref[g] = total_ref[g]

    @pl.when(is_owner)
    def _():
        for i in range(len(x_peers + c_peers)):
            remote(rows_ref, rows_ref, es.at[i], er.at[0, 0], right).wait_send()
        own.wait()

    if nc == 2:

        @pl.when(jnp.logical_and(in_column, jnp.logical_not(is_owner)))
        def _():
            remote(rows_ref, rows_ref, es.at[nx - 1], er.at[0, 0], right).wait_send()

        waits_rows = jnp.logical_not(in_column)
    else:
        waits_rows = jnp.logical_not(is_owner)

    @pl.when(waits_rows)
    def _():
        for k in steps:

            @pl.when(present(k))
            def _():
                for d in range(ny):
                    spot = rows_ref.at[source(k, d)]
                    remote(spot, spot, es.at[0], er.at[d, k], right).wait_recv()

    for k in steps:

        @pl.when(present(k))
        def _():
            if k == 0 or k % 2:

                @pl.when(has_right)
                def _():
                    along(k, True).wait_send()

            if k == 0 or k % 2 == 0:

                @pl.when(has_left)
                def _():
                    along(k, False).wait_send()

            for d in range(1, ny):
                across(k, d).wait_send()

    for i in range(chunks):
        for d in range(nx):
            if nc == 2:
                core_copy(i, d).wait_send()
            if d:
                pair_copy(i, d).wait_send()
    for copy in g_copies:
        copy.wait()


def front(masked, density, grid_count, tile_count):
    batch, cols = masked.shape
    rows = density.shape[0]
    nz, ny = grid_split(grid_count)
    nx, nc = tile_split(tile_count)
    slab = batch // tile_count
    width = min(rows, 512)
    chunks = rows // width
    dma = pltpu.SemaphoreType.DMA
    return pl.pallas_call(
        functools.partial(front_kernel, grid_count, tile_count),
        out_shape=(
            jax.ShapeDtypeStruct((grid_count, slab, rows), bf16),
            jax.ShapeDtypeStruct((grid_count, batch, rows), bf16),
        ),
        in_specs=[vmem(), pl.BlockSpec(memory_space=pl.ANY)],
        out_specs=(vmem(), vmem()),
        scratch_shapes=[
            pltpu.VMEM((grid_count, batch, cols), bf16),
            pltpu.VMEM((rows, cols), bf16),
            pltpu.VMEM((chunks, grid_count, nx, nc, slab, width), bf16),
            pltpu.VMEM((chunks, grid_count, nx, slab, width), bf16),
            pltpu.VMEM((chunks, nx, grid_count, slab, width), bf16),
            pltpu.VMEM((chunks, nx, grid_count, slab, width), bf16),
            pltpu.VMEM((grid_count, slab, rows), bf16),
            dma((2, nz)),
            dma((2, nz)),
            dma((ny, 2 * nz)),
            dma((ny, 2 * nz)),
            dma((nx,)),
            dma((ny, 2 * nz)),
            dma,
            dma((chunks,)),
            dma((chunks, nx)),
            dma((chunks, nx)),
            dma((chunks, nx)),
            dma((chunks, nx)),
            dma((grid_count,)),
            dma((grid_count,)),
        ],
        compiler_params=params(0),
    )(masked, density)


def finish_kernel(
    grid_count,
    tile_count,
    pot_ref,
    lmo_hbm,
    mask_ref,
    all_ref,
    lmo_ref,
    got_ref,
    flat_ref,
    send_ref,
    part_ref,
    own_ref,
    lmo_sem,
    vs,
    vr,
    ws,
    wr,
    gs,
    gr,
):
    g, t = lax.axis_index("grid"), lax.axis_index("tile")
    load = pltpu.make_async_copy(lmo_hbm, lmo_ref, lmo_sem)
    load.start()
    t_peers = [(g, lax.rem(t + d, tile_count)) for d in range(1, tile_count)]
    g_peers = [(lax.rem(g + d, grid_count), t) for d in range(1, grid_count)]
    greet(t_peers + g_peers)
    cols = mask_ref.shape[0]
    slab = pot_ref.shape[1]
    block = pot_ref.shape[2]
    strip = own_ref.shape[1]

    v_copies = []
    for d in range(1, tile_count):
        target = lax.rem(t + d, tile_count)
        copy = remote(
            pot_ref.at[pl.ds(target * cols, cols)],
            got_ref.at[t],
            vs.at[d],
            vr.at[d],
            t_peers[d - 1],
        )
        copy.start()
        v_copies.append(copy)
    got_ref[t] = pot_ref[pl.ds(t * cols, cols)]
    for copy in v_copies:
        copy.wait()
    for i in range(tile_count):
        for m in range(cols):
            flat_ref[m, i * slab : (i + 1) * slab, :] = got_ref[i, m].astype(f32)
    load.wait()
    for s in range(tile_count):
        lanes = slice(s * strip, (s + 1) * strip)
        total = None
        for m in range(cols):
            term = mask_ref[m : m + 1, lanes] * jnp.dot(
                flat_ref[m].astype(bf16),
                lmo_ref[m * block : (m + 1) * block, lanes],
                preferred_element_type=f32,
            )
            total = term if total is None else total + term
        send_ref[s] = total.astype(bf16)
    w_copies = []
    for d in range(1, tile_count):
        target = lax.rem(t + d, tile_count)
        copy = remote(
            send_ref.at[target], part_ref.at[d], ws.at[d], wr.at[d], t_peers[d - 1]
        )
        copy.start()
        w_copies.append(copy)
    total = send_ref[t].astype(f32)
    for d, copy in enumerate(w_copies):
        copy.wait()
        total = total + part_ref[d + 1].astype(f32)
    own_ref[...] = total.astype(bf16)
    g_copies = []
    for d in range(1, grid_count):
        copy = remote(own_ref, all_ref.at[g], gs.at[d], gr.at[d], g_peers[d - 1])
        copy.start()
        g_copies.append(copy)
    all_ref[g] = own_ref[...]
    for copy in g_copies:
        copy.wait()


def finish(potential, lmo_coeffs, mask, batch, grid_count, tile_count):
    blocks, slab, block = potential.shape
    cols = blocks // tile_count
    total = lmo_coeffs.shape[1]
    strip = total // tile_count
    dma = pltpu.SemaphoreType.DMA
    return pl.pallas_call(
        functools.partial(finish_kernel, grid_count, tile_count),
        out_shape=jax.ShapeDtypeStruct((grid_count, batch, strip), bf16),
        in_specs=[vmem(), pl.BlockSpec(memory_space=pl.ANY), vmem()],
        out_specs=vmem(),
        scratch_shapes=[
            pltpu.VMEM(lmo_coeffs.shape, bf16),
            pltpu.VMEM((tile_count, cols, slab, block), bf16),
            pltpu.VMEM((cols, batch, block), f32),
            pltpu.VMEM((tile_count, batch, strip), bf16),
            pltpu.VMEM((tile_count, batch, strip), bf16),
            pltpu.VMEM((batch, strip), bf16),
            dma,
            dma((tile_count,)),
            dma((tile_count,)),
            dma((tile_count,)),
            dma((tile_count,)),
            dma((grid_count,)),
            dma((grid_count,)),
        ],
        compiler_params=params(2),
    )(potential, lmo_coeffs, mask)


def shards(
    point_values,
    sig_blocks,
    density,
    coulomb_core,
    screen_mask,
    ao_centers,
    ao_widths,
    point_coords,
    lmo_coeffs,
    domain_blocks,
):
    grid_count = lax.axis_size("grid")
    tile_count = lax.axis_size("tile")
    panel = lax.axis_index("tile")
    own_rows, own_cols = density.shape
    points = point_values.shape[0]
    block_size = coulomb_core.shape[0]
    total_aos = ao_widths.shape[0]
    all_blocks = total_aos // block_size
    col_blocks = own_cols // block_size
    slab = points // tile_count
    block_ids = jnp.arange(all_blocks, dtype=jnp.int32)
    named = jnp.any(sig_blocks[0][:, None] == block_ids[None, :], axis=0)
    first_col = panel * col_blocks
    named_cols = lax.dynamic_slice_in_dim(named.astype(f32), first_col, col_blocks, 0)
    col_mask = jnp.repeat(named_cols, block_size)
    masked = point_values * col_mask[None, :].astype(bf16)
    summed, row_values = front(masked, density, grid_count, tile_count)
    row_blocks = own_rows // block_size
    term = summed.astype(f32).reshape(grid_count, slab, row_blocks, block_size)
    term = jnp.transpose(term, (0, 2, 1, 3)).reshape(all_blocks, slab, block_size)
    coords = lax.dynamic_slice_in_dim(point_coords, panel * slab, slab, 1)
    offsets = (
        ao_centers.reshape(3, all_blocks, 1, block_size) - coords.reshape(3, 1, slab, 1)
    )
    coefficient = 1.0 / jnp.sqrt(
        jnp.sum(offsets * offsets, axis=0) + ao_widths.reshape(all_blocks, 1, block_size)
    )
    scaled = coefficient * named.astype(f32)[:, None, None]
    weighted = (scaled * term).astype(bf16)
    screened = jnp.einsum(
        "kj,jpa->kpa", screen_mask.astype(bf16), weighted, preferred_element_type=f32
    ).astype(bf16)
    mixed = jnp.einsum(
        "kpc,ac->kpa", screened, coulomb_core, preferred_element_type=f32
    )
    potential = (scaled * mixed).astype(bf16)
    local_ids = first_col + jnp.arange(col_blocks, dtype=jnp.int32)
    in_domain = jnp.any(domain_blocks[:, :, None] == local_ids[None, None, :], axis=1)
    strip_width = lmo_coeffs.shape[1] // domain_blocks.shape[0]
    mask = jnp.repeat(jnp.transpose(in_domain).astype(f32), strip_width, axis=1)
    weights = finish(potential, lmo_coeffs, mask, points, grid_count, tile_count)
    return lax.dot_general(
        weights.reshape(grid_count * points, weights.shape[2]),
        row_values.reshape(grid_count * points, own_rows),
        (((0,), (0,)), ((), ())),
        preferred_element_type=f32,
    ).astype(bf16)


def solution(mesh):
    in_specs = (
        P("grid", "tile"),
        P("grid", None),
        P("grid", "tile"),
        P(),
        P(),
        P(),
        P(),
        P(None, "grid"),
        P("tile", None),
        P(),
    )
    out_specs = P("tile", "grid")
    return jax.shard_map(shards, mesh=mesh, in_specs=in_specs, out_specs=out_specs, check_vma=False)
```

```python
import functools
import math

import jax
import jax.numpy as jnp
from jax import lax
from jax.experimental import pallas as pl
from jax.experimental.pallas import tpu as pltpu
from jax.sharding import PartitionSpec as P

MESH = pl.DeviceIdType.MESH
VMEM_LIMIT = 60 * 1024 * 1024
f32 = jnp.float32
bf16 = jnp.bfloat16


def grid_split(grid_count):
    inner = max(1, math.isqrt(max(1, grid_count // 2)))
    while grid_count % inner:
        inner -= 1
    return grid_count // inner, inner


def tile_split(tile_count):
    inner = 2 if tile_count % 2 == 0 else 1
    return tile_count // inner, inner


def remote(src, dst, send_sem, recv_sem, device):
    return pltpu.make_async_remote_copy(
        src_ref=src,
        dst_ref=dst,
        send_sem=send_sem,
        recv_sem=recv_sem,
        device_id=device,
        device_id_type=MESH,
    )


def greet(devices):
    barrier = pltpu.get_barrier_semaphore()
    for device in devices:
        pl.semaphore_signal(barrier, inc=1, device_id=device, device_id_type=MESH)
    pl.semaphore_wait(barrier, len(devices))


def params(collective_id):
    return pltpu.CompilerParams(
        collective_id=collective_id, has_side_effects=True, vmem_limit_bytes=VMEM_LIMIT
    )


def vmem():
    return pl.BlockSpec(memory_space=pltpu.VMEM)


def listed(table_ref, row, block_id):
    flag = jnp.float32(0.0)
    for i in range(table_ref.shape[1]):
        flag = jnp.where(table_ref[row, i] == block_id, jnp.float32(1.0), flag)
    return flag


def front_kernel(
    block_size,
    grid_count,
    tile_count,
    sig_ref,
    value_ref,
    density_hbm,
    out_ref,
    rows_ref,
    x_ref,
    all_ref,
    density_ref,
    part_ref,
    sibling_ref,
    pair_ref,
    peer_ref,
    total_ref,
    zs,
    zr,
    ys,
    yr,
    es,
    er,
    local_sem,
    ds,
    cs,
    cr,
    xs,
    xr,
    gs,
    gr,
):
    chunks, slab, width = part_ref.shape[0], part_ref.shape[4], part_ref.shape[5]
    loads = [
        pltpu.make_async_copy(
            density_hbm.at[pl.ds(i * width, width)],
            density_ref.at[pl.ds(i * width, width)],
            ds.at[i],
        )
        for i in range(chunks)
    ]
    g, t = lax.axis_index("grid"), lax.axis_index("tile")
    nz, ny = grid_split(grid_count)
    nx, nc = tile_split(tile_count)
    z, y = g // ny, g % ny
    x, c = t // nc, t % nc
    cols = x_ref.shape[1]
    rows = rows_ref.shape[2]
    offset = pl.multiple_of((g * rows) % cols, rows)
    owner = (g * rows) // cols
    is_owner = owner == t
    in_column = owner % nc == c
    has_left, has_right = z > 0, z < nz - 1
    left = (lax.rem(z + nz - 1, nz) * ny + y, t)
    right = (lax.rem(z + 1, nz) * ny + y, t)
    y_peers = [(z * ny + lax.rem(y + d, ny), t) for d in range(1, ny)]
    x_peers = [(g, lax.rem(x + d, nx) * nc + c) for d in range(1, nx)]
    c_peers = [(g, x * nc + (1 - c))] if nc == 2 else []
    g_peers = [(lax.rem(g + d, grid_count), t) for d in range(1, grid_count)]
    for m in range(cols // block_size):
        lanes = slice(m * block_size, (m + 1) * block_size)
        flag = listed(sig_ref, 0, t * (cols // block_size) + m)
        x_ref[:, lanes] = (value_ref[:, lanes].astype(f32) * flag).astype(bf16)
    greet(g_peers + x_peers + c_peers)

    def present(k):
        if k == 0:
            return z >= 0
        step = (k + 1) // 2
        return z >= step if k % 2 else z <= nz - 1 - step

    def source(k, d):
        step = (k + 1) // 2
        line = lax.rem(z + nz - step, nz) if k % 2 else lax.rem(z + step, nz)
        return line * ny + lax.rem(y + ny - d, ny)

    def block(k, d):
        return x_ref if k == 0 and d == 0 else all_ref.at[source(k, d)]

    def along(k, to_right):
        step = (k + 1) // 2
        lane = 0 if to_right else 1
        return remote(
            block(k, 0),
            all_ref.at[source(k, 0)],
            zs.at[lane, step],
            zr.at[lane, step],
            right if to_right else left,
        )

    def across(k, d):
        return remote(
            block(k, 0), all_ref.at[source(k, 0)], ys.at[d, k], yr.at[d, k], y_peers[d - 1]
        )

    def arrived(k, d, sends, recvs):
        spot = all_ref.at[source(k, d)]
        remote(spot, spot, sends, recvs, right).wait_recv()

    def share(k, d):
        for i, peer in enumerate(x_peers + c_peers):
            remote(
                block(k, d).at[:, pl.ds(offset, rows)],
                rows_ref.at[source(k, d)],
                es.at[i],
                er.at[d, k],
                peer,
            ).start()

    steps = range(2 * nz - 1)

    def send_block(k):
        if k == 0 or k % 2:

            @pl.when(has_right)
            def _():
                along(k, True).start()

        if k == 0 or k % 2 == 0:

            @pl.when(has_left)
            def _():
                along(k, False).start()

        for d in range(1, ny):
            across(k, d).start()

        @pl.when(is_owner)
        def _():
            share(k, 0)

    def take_across(k):
        @pl.when(present(k))
        def _():
            for d in range(1, ny):
                arrived(k, d, ys.at[d, k], yr.at[d, k])

                @pl.when(is_owner)
                def _():
                    share(k, d)

    batch = x_ref.shape[0]
    halves = 2 if nz % 4 == 0 else 1
    part_rows = grid_count // halves
    half = z // (nz // halves)

    def product(i, h):
        if h == 0:
            loads[i].wait()
        group = pl.ds(lax.rem(half + h, halves) * part_rows, part_rows)
        value = lax.dot_general(
            all_ref[group].reshape(part_rows * batch, cols),
            density_ref[i * width : (i + 1) * width, :],
            (((1,), (1,)), ((), ())),
            preferred_element_type=f32,
        )
        if slab % 8 == 0:
            part_ref[i, group] = value.reshape(part_rows, nx, nc, slab, width).astype(bf16)
        else:
            first = lax.rem(half + h, halves) * part_rows
            for n in range(part_rows * batch // slab):
                part_ref[i, first + n // (nx * nc), n // nc % nx, n % nc] = value[
                    n * slab : (n + 1) * slab
                ].astype(bf16)

    early = (chunks + 1) // 2
    send_block(0)
    keep = pltpu.make_async_copy(x_ref, all_ref.at[g], local_sem)
    keep.start()
    for load in loads:
        load.start()
    for step in range(1, nz):
        for k in (2 * step - 1, 2 * step):

            @pl.when(present(k))
            def _():
                lane = 0 if k % 2 else 1
                arrived(k, 0, zs.at[lane, step - 1], zr.at[lane, step - 1])
                send_block(k)

        if halves == 2 and step == nz // 2 + 1:
            for i in range(early, chunks):
                product(i, 0)
        if step == 1:
            take_across(0)
        else:
            take_across(2 * step - 3)
            take_across(2 * step - 2)
        if halves == 2 and step == nz // 2:
            keep.wait()
            for i in range(early):
                product(i, 0)
    if nz > 1:
        take_across(2 * nz - 3)
        take_across(2 * nz - 2)
    else:
        take_across(0)
    if halves == 1:
        keep.wait()
    order = list(range(1, nx)) + [0]

    def core_copy(i, d):
        column = lax.rem(x + d, nx)
        return remote(
            part_ref.at[i, :, column, 1 - c],
            sibling_ref.at[i, :, column],
            cs.at[i, d],
            cr.at[i, d],
            c_peers[0],
        )

    def pair_copy(i, d):
        return remote(
            pair_ref.at[i, d], peer_ref.at[i, d], xs.at[i, d], xr.at[i, d], x_peers[d - 1]
        )

    def exchange(i):
        for d in order:
            column = lax.rem(x + d, nx)
            if nc == 2:
                core_copy(i, d).wait_recv()

            @pl.loop(0, grid_count)
            def _(n):
                value = part_ref[i, n, column, c].astype(f32)
                if nc == 2:
                    value = value + sibling_ref[i, n, column].astype(f32)
                pair_ref[i, d, n] = value.astype(bf16)

            if d:
                pair_copy(i, d).start()

    def pass_rows():
        @pl.when(jnp.logical_not(is_owner))
        def _():
            for k in steps:

                @pl.when(present(k))
                def _():
                    for d in range(ny):
                        spot = rows_ref.at[source(k, d)]
                        pass_on = remote(
                            spot, spot, es.at[nx - 1], er.at[d, k], (c_peers or [right])[0]
                        )
                        if nc == 2:

                            @pl.when(in_column)
                            def _():
                                pass_on.wait_recv()
                                pass_on.start()

    own = pltpu.make_async_copy(all_ref.at[:, :, pl.ds(offset, rows)], rows_ref, local_sem)

    @pl.when(is_owner)
    def _():
        own.start()

    for i in range(chunks):
        product(i, halves - 1)
        if nc == 2:
            for d in order:
                core_copy(i, d).start()
        if i == 0:
            pass_rows()
        else:
            exchange(i - 1)
    exchange(chunks - 1)

    for i in range(chunks):
        for d in range(1, nx):
            pair_copy(i, d).wait_recv()

        @pl.loop(0, grid_count)
        def _(n):
            value = pair_ref[i, 0, n].astype(f32)
            for d in range(1, nx):
                value = value + peer_ref[i, d, n].astype(f32)
            total_ref[n, :, i * width : (i + 1) * width] = value.astype(bf16)

    g_copies = []
    for d in range(1, grid_count):
        target = lax.rem(g + d, grid_count)
        copy = remote(
            total_ref.at[target], out_ref.at[g], gs.at[d], gr.at[d], g_peers[d - 1]
        )
        copy.start()
        g_copies.append(copy)
    out_ref[g] = total_ref[g]

    @pl.when(is_owner)
    def _():
        for i in range(len(x_peers + c_peers)):
            remote(rows_ref, rows_ref, es.at[i], er.at[0, 0], right).wait_send()
        own.wait()

    if nc == 2:

        @pl.when(jnp.logical_and(in_column, jnp.logical_not(is_owner)))
        def _():
            remote(rows_ref, rows_ref, es.at[nx - 1], er.at[0, 0], right).wait_send()

        waits_rows = jnp.logical_not(in_column)
    else:
        waits_rows = jnp.logical_not(is_owner)

    @pl.when(waits_rows)
    def _():
        for k in steps:

            @pl.when(present(k))
            def _():
                for d in range(ny):
                    spot = rows_ref.at[source(k, d)]
                    remote(spot, spot, es.at[0], er.at[d, k], right).wait_recv()

    for k in steps:

        @pl.when(present(k))
        def _():
            if k == 0 or k % 2:

                @pl.when(has_right)
                def _():
                    along(k, True).wait_send()

            if k == 0 or k % 2 == 0:

                @pl.when(has_left)
                def _():
                    along(k, False).wait_send()

            for d in range(1, ny):
                across(k, d).wait_send()

    for i in range(chunks):
        for d in range(nx):
            if nc == 2:
                core_copy(i, d).wait_send()
            if d:
                pair_copy(i, d).wait_send()
    for copy in g_copies:
        copy.wait()


def smem():
    return pl.BlockSpec(memory_space=pltpu.SMEM)


def front(sig_blocks, values, density, block_size, grid_count, tile_count):
    batch, cols = values.shape
    rows = density.shape[0]
    nz, ny = grid_split(grid_count)
    nx, nc = tile_split(tile_count)
    slab = batch // tile_count
    width = min(rows, 512)
    chunks = rows // width
    dma = pltpu.SemaphoreType.DMA
    return pl.pallas_call(
        functools.partial(front_kernel, block_size, grid_count, tile_count),
        out_shape=(
            jax.ShapeDtypeStruct((grid_count, slab, rows), bf16),
            jax.ShapeDtypeStruct((grid_count, batch, rows), bf16),
        ),
        in_specs=[smem(), vmem(), pl.BlockSpec(memory_space=pl.ANY)],
        out_specs=(vmem(), vmem()),
        scratch_shapes=[
            pltpu.VMEM((batch, cols), bf16),
            pltpu.VMEM((grid_count, batch, cols), bf16),
            pltpu.VMEM((rows, cols), bf16),
            pltpu.VMEM((chunks, grid_count, nx, nc, slab, width), bf16),
            pltpu.VMEM((chunks, grid_count, nx, slab, width), bf16),
            pltpu.VMEM((chunks, nx, grid_count, slab, width), bf16),
            pltpu.VMEM((chunks, nx, grid_count, slab, width), bf16),
            pltpu.VMEM((grid_count, slab, rows), bf16),
            dma((2, nz)),
            dma((2, nz)),
            dma((ny, 2 * nz)),
            dma((ny, 2 * nz)),
            dma((nx,)),
            dma((ny, 2 * nz)),
            dma,
            dma((chunks,)),
            dma((chunks, nx)),
            dma((chunks, nx)),
            dma((chunks, nx)),
            dma((chunks, nx)),
            dma((grid_count,)),
            dma((grid_count,)),
        ],
        compiler_params=params(0),
    )(sig_blocks, values, density)


def finish_kernel(
    grid_count,
    tile_count,
    pot_ref,
    lmo_hbm,
    domain_ref,
    all_ref,
    lmo_ref,
    got_ref,
    flat_ref,
    send_ref,
    part_ref,
    own_ref,
    lmo_sem,
    vs,
    vr,
    ws,
    wr,
    gs,
    gr,
):
    g, t = lax.axis_index("grid"), lax.axis_index("tile")
    load = pltpu.make_async_copy(lmo_hbm, lmo_ref, lmo_sem)
    load.start()
    t_peers = [(g, lax.rem(t + d, tile_count)) for d in range(1, tile_count)]
    g_peers = [(lax.rem(g + d, grid_count), t) for d in range(1, grid_count)]
    greet(t_peers + g_peers)
    cols = got_ref.shape[1]
    strips = domain_ref.shape[0]
    slab = pot_ref.shape[1]
    block = pot_ref.shape[2]
    strip = own_ref.shape[1]

    v_copies = []
    for d in range(1, tile_count):
        target = lax.rem(t + d, tile_count)
        copy = remote(
            pot_ref.at[pl.ds(target * cols, cols)],
            got_ref.at[t],
            vs.at[d],
            vr.at[d],
            t_peers[d - 1],
        )
        copy.start()
        v_copies.append(copy)
    got_ref[t] = pot_ref[pl.ds(t * cols, cols)]
    flags = [[listed(domain_ref, s, t * cols + m) for m in range(cols)] for s in range(strips)]
    for copy in v_copies:
        copy.wait()
    for i in range(tile_count):
        for m in range(cols):
            flat_ref[m, i * slab : (i + 1) * slab, :] = got_ref[i, m].astype(f32)
    load.wait()
    width = lmo_ref.shape[1] // strips
    per_tile = strips // tile_count
    for s in range(strips):
        lanes = slice(s * width, (s + 1) * width)
        total = None
        for m in range(cols):
            term = flags[s][m] * jnp.dot(
                flat_ref[m].astype(bf16),
                lmo_ref[m * block : (m + 1) * block, lanes],
                preferred_element_type=f32,
            )
            total = term if total is None else total + term
        first = s % per_tile * width
        send_ref[s // per_tile, :, first : first + width] = total.astype(bf16)
    w_copies = []
    for d in range(1, tile_count):
        target = lax.rem(t + d, tile_count)
        copy = remote(
            send_ref.at[target], part_ref.at[d], ws.at[d], wr.at[d], t_peers[d - 1]
        )
        copy.start()
        w_copies.append(copy)
    total = send_ref[t].astype(f32)
    for d, copy in enumerate(w_copies):
        copy.wait()
        total = total + part_ref[d + 1].astype(f32)
    own_ref[...] = total.astype(bf16)
    g_copies = []
    for d in range(1, grid_count):
        copy = remote(own_ref, all_ref.at[g], gs.at[d], gr.at[d], g_peers[d - 1])
        copy.start()
        g_copies.append(copy)
    all_ref[g] = own_ref[...]
    for copy in g_copies:
        copy.wait()


def finish(potential, lmo_coeffs, domain_blocks, batch, grid_count, tile_count):
    blocks, slab, block = potential.shape
    cols = blocks // tile_count
    total = lmo_coeffs.shape[1]
    strip = total // tile_count
    dma = pltpu.SemaphoreType.DMA
    return pl.pallas_call(
        functools.partial(finish_kernel, grid_count, tile_count),
        out_shape=jax.ShapeDtypeStruct((grid_count, batch, strip), bf16),
        in_specs=[vmem(), pl.BlockSpec(memory_space=pl.ANY), smem()],
        out_specs=vmem(),
        scratch_shapes=[
            pltpu.VMEM(lmo_coeffs.shape, bf16),
            pltpu.VMEM((tile_count, cols, slab, block), bf16),
            pltpu.VMEM((cols, batch, block), f32),
            pltpu.VMEM((tile_count, batch, strip), bf16),
            pltpu.VMEM((tile_count, batch, strip), bf16),
            pltpu.VMEM((batch, strip), bf16),
            dma,
            dma((tile_count,)),
            dma((tile_count,)),
            dma((tile_count,)),
            dma((tile_count,)),
            dma((grid_count,)),
            dma((grid_count,)),
        ],
        compiler_params=params(2),
    )(potential, lmo_coeffs, domain_blocks)


def shards(
    point_values,
    sig_blocks,
    density,
    coulomb_core,
    screen_mask,
    ao_centers,
    ao_widths,
    point_coords,
    lmo_coeffs,
    domain_blocks,
):
    grid_count = lax.axis_size("grid")
    tile_count = lax.axis_size("tile")
    panel = lax.axis_index("tile")
    own_rows, own_cols = density.shape
    points = point_values.shape[0]
    block_size = coulomb_core.shape[0]
    total_aos = ao_widths.shape[0]
    all_blocks = total_aos // block_size
    slab = points // tile_count
    block_ids = jnp.arange(all_blocks, dtype=jnp.int32)
    named = jnp.any(sig_blocks[0][:, None] == block_ids[None, :], axis=0)
    summed, row_values = front(
        sig_blocks, point_values, density, block_size, grid_count, tile_count
    )
    row_blocks = own_rows // block_size
    term = summed.astype(f32).reshape(grid_count, slab, row_blocks, block_size)
    term = jnp.transpose(term, (0, 2, 1, 3)).reshape(all_blocks, slab, block_size)
    coords = lax.dynamic_slice_in_dim(point_coords, panel * slab, slab, 1)
    offsets = (
        ao_centers.reshape(3, all_blocks, 1, block_size) - coords.reshape(3, 1, slab, 1)
    )
    coefficient = 1.0 / jnp.sqrt(
        jnp.sum(offsets * offsets, axis=0) + ao_widths.reshape(all_blocks, 1, block_size)
    )
    scaled = coefficient * named.astype(f32)[:, None, None]
    weighted = (scaled * term).astype(bf16)
    screened = jnp.einsum(
        "kj,jpa->kpa", screen_mask.astype(bf16), weighted, preferred_element_type=f32
    ).astype(bf16)
    mixed = jnp.einsum(
        "kpc,ac->kpa", screened, coulomb_core, preferred_element_type=f32
    )
    potential = (scaled * mixed).astype(bf16)
    weights = finish(potential, lmo_coeffs, domain_blocks, points, grid_count, tile_count)
    return lax.dot_general(
        weights.reshape(grid_count * points, weights.shape[2]),
        row_values.reshape(grid_count * points, own_rows),
        (((0,), (0,)), ((), ())),
        preferred_element_type=f32,
    ).astype(bf16)


def solution(mesh):
    in_specs = (
        P("grid", "tile"),
        P("grid", None),
        P("grid", "tile"),
        P(),
        P(),
        P(),
        P(),
        P(None, "grid"),
        P("tile", None),
        P(),
    )
    out_specs = P("tile", "grid")
    return jax.shard_map(shards, mesh=mesh, in_specs=in_specs, out_specs=out_specs, check_vma=False)
```

```python
import functools
import math

import jax
import jax.numpy as jnp
from jax import lax
from jax.experimental import pallas as pl
from jax.experimental.pallas import tpu as pltpu
from jax.sharding import PartitionSpec as P

MESH = pl.DeviceIdType.MESH
VMEM_LIMIT = 60 * 1024 * 1024
f32 = jnp.float32
bf16 = jnp.bfloat16


def grid_split(grid_count):
    inner = max(1, math.isqrt(max(1, grid_count // 2)))
    while grid_count % inner:
        inner -= 1
    return grid_count // inner, inner


def tile_split(tile_count):
    inner = 2 if tile_count % 2 == 0 else 1
    return tile_count // inner, inner


def remote(src, dst, send_sem, recv_sem, device):
    return pltpu.make_async_remote_copy(
        src_ref=src,
        dst_ref=dst,
        send_sem=send_sem,
        recv_sem=recv_sem,
        device_id=device,
        device_id_type=MESH,
    )


def greet(devices, work=None):
    barrier = pltpu.get_barrier_semaphore()
    for device in devices:
        pl.semaphore_signal(barrier, inc=1, device_id=device, device_id_type=MESH)
    if work is not None:
        work()
    pl.semaphore_wait(barrier, len(devices))


def params(collective_id):
    return pltpu.CompilerParams(
        collective_id=collective_id, has_side_effects=True, vmem_limit_bytes=VMEM_LIMIT
    )


def vmem():
    return pl.BlockSpec(memory_space=pltpu.VMEM)


def listed(table_ref, row, block_id):
    flag = jnp.float32(0.0)
    for i in range(table_ref.shape[1]):
        flag = jnp.where(table_ref[row, i] == block_id, jnp.float32(1.0), flag)
    return flag


def front_kernel(
    block_size,
    grid_count,
    tile_count,
    sig_ref,
    value_ref,
    density_hbm,
    out_ref,
    rows_ref,
    x_ref,
    all_ref,
    density_ref,
    part_ref,
    sibling_ref,
    pair_ref,
    peer_ref,
    total_ref,
    zs,
    zr,
    ys,
    yr,
    es,
    er,
    local_sem,
    ds,
    cs,
    cr,
    xs,
    xr,
    gs,
    gr,
):
    chunks, slab, width = part_ref.shape[0], part_ref.shape[4], part_ref.shape[5]
    loads = [
        pltpu.make_async_copy(
            density_hbm.at[pl.ds(i * width, width)],
            density_ref.at[pl.ds(i * width, width)],
            ds.at[i],
        )
        for i in range(chunks)
    ]
    g, t = lax.axis_index("grid"), lax.axis_index("tile")
    nz, ny = grid_split(grid_count)
    nx, nc = tile_split(tile_count)
    z, y = g // ny, g % ny
    x, c = t // nc, t % nc
    cols = x_ref.shape[1]
    rows = rows_ref.shape[2]
    offset = pl.multiple_of((g * rows) % cols, rows)
    owner = (g * rows) // cols
    is_owner = owner == t
    in_column = owner % nc == c
    has_left, has_right = z > 0, z < nz - 1
    left = (lax.rem(z + nz - 1, nz) * ny + y, t)
    right = (lax.rem(z + 1, nz) * ny + y, t)
    y_peers = [(z * ny + lax.rem(y + d, ny), t) for d in range(1, ny)]
    x_peers = [(g, lax.rem(x + d, nx) * nc + c) for d in range(1, nx)]
    c_peers = [(g, x * nc + (1 - c))] if nc == 2 else []
    g_peers = [(lax.rem(g + d, grid_count), t) for d in range(1, grid_count)]

    def make_mask():
        for m in range(cols // block_size):
            lanes = slice(m * block_size, (m + 1) * block_size)
            flag = listed(sig_ref, 0, t * (cols // block_size) + m)
            x_ref[:, lanes] = (value_ref[:, lanes].astype(f32) * flag).astype(bf16)

    greet(g_peers + x_peers + c_peers, make_mask)

    def present(k):
        if k == 0:
            return z >= 0
        step = (k + 1) // 2
        return z >= step if k % 2 else z <= nz - 1 - step

    def source(k, d):
        step = (k + 1) // 2
        line = lax.rem(z + nz - step, nz) if k % 2 else lax.rem(z + step, nz)
        return line * ny + lax.rem(y + ny - d, ny)

    def block(k, d):
        return x_ref if k == 0 and d == 0 else all_ref.at[source(k, d)]

    def along(k, to_right):
        step = (k + 1) // 2
        lane = 0 if to_right else 1
        return remote(
            block(k, 0),
            all_ref.at[source(k, 0)],
            zs.at[lane, step],
            zr.at[lane, step],
            right if to_right else left,
        )

    def across(k, d):
        return remote(
            block(k, 0), all_ref.at[source(k, 0)], ys.at[d, k], yr.at[d, k], y_peers[d - 1]
        )

    def arrived(k, d, sends, recvs):
        spot = all_ref.at[source(k, d)]
        remote(spot, spot, sends, recvs, right).wait_recv()

    def share(k, d):
        for i, peer in enumerate(x_peers + c_peers):
            remote(
                block(k, d).at[:, pl.ds(offset, rows)],
                rows_ref.at[source(k, d)],
                es.at[i],
                er.at[d, k],
                peer,
            ).start()

    steps = range(2 * nz - 1)

    def send_block(k):
        if k == 0 or k % 2:

            @pl.when(has_right)
            def _():
                along(k, True).start()

        if k == 0 or k % 2 == 0:

            @pl.when(has_left)
            def _():
                along(k, False).start()

        for d in range(1, ny):
            across(k, d).start()

        @pl.when(is_owner)
        def _():
            share(k, 0)

    def take_across(k):
        @pl.when(present(k))
        def _():
            for d in range(1, ny):
                arrived(k, d, ys.at[d, k], yr.at[d, k])

                @pl.when(is_owner)
                def _():
                    share(k, d)

    batch = x_ref.shape[0]

    def product(i):
        loads[i].wait()
        value = lax.dot_general(
            all_ref[...].reshape(grid_count * batch, cols),
            density_ref[i * width : (i + 1) * width, :],
            (((1,), (1,)), ((), ())),
            preferred_element_type=f32,
        )
        if slab % 8 == 0:
            part_ref[i] = value.reshape(grid_count, nx, nc, slab, width).astype(bf16)
        else:
            for n in range(grid_count * batch // slab):
                part_ref[i, n // (nx * nc), n // nc % nx, n % nc] = value[
                    n * slab : (n + 1) * slab
                ].astype(bf16)

    send_block(0)
    keep = pltpu.make_async_copy(x_ref, all_ref.at[g], local_sem)
    keep.start()
    for load in loads:
        load.start()
    for step in range(1, nz):
        for k in (2 * step - 1, 2 * step):

            @pl.when(present(k))
            def _():
                lane = 0 if k % 2 else 1
                arrived(k, 0, zs.at[lane, step - 1], zr.at[lane, step - 1])
                send_block(k)

        if step == 1:
            take_across(0)
        else:
            take_across(2 * step - 3)
            take_across(2 * step - 2)
    if nz > 1:
        take_across(2 * nz - 3)
        take_across(2 * nz - 2)
    else:
        take_across(0)
    keep.wait()
    order = list(range(1, nx)) + [0]

    def core_copy(i, d):
        column = lax.rem(x + d, nx)
        return remote(
            part_ref.at[i, :, column, 1 - c],
            sibling_ref.at[i, :, column],
            cs.at[i, d],
            cr.at[i, d],
            c_peers[0],
        )

    def pair_copy(i, d):
        return remote(
            pair_ref.at[i, d], peer_ref.at[i, d], xs.at[i, d], xr.at[i, d], x_peers[d - 1]
        )

    def exchange(i):
        for d in order:
            column = lax.rem(x + d, nx)
            if nc == 2:
                core_copy(i, d).wait_recv()

            @pl.loop(0, grid_count)
            def _(n):
                value = part_ref[i, n, column, c].astype(f32)
                if nc == 2:
                    value = value + sibling_ref[i, n, column].astype(f32)
                pair_ref[i, d, n] = value.astype(bf16)

            if d:
                pair_copy(i, d).start()

    def pass_rows():
        @pl.when(jnp.logical_not(is_owner))
        def _():
            for k in steps:

                @pl.when(present(k))
                def _():
                    for d in range(ny):
                        spot = rows_ref.at[source(k, d)]
                        pass_on = remote(
                            spot, spot, es.at[nx - 1], er.at[d, k], (c_peers or [right])[0]
                        )
                        if nc == 2:

                            @pl.when(in_column)
                            def _():
                                pass_on.wait_recv()
                                pass_on.start()

    own = pltpu.make_async_copy(all_ref.at[:, :, pl.ds(offset, rows)], rows_ref, local_sem)

    @pl.when(is_owner)
    def _():
        own.start()

    for i in range(chunks):
        product(i)
        if nc == 2:
            for d in order:
                core_copy(i, d).start()
        if i == 0:
            pass_rows()
        else:
            exchange(i - 1)
    exchange(chunks - 1)

    for i in range(chunks):
        for d in range(1, nx):
            pair_copy(i, d).wait_recv()

        @pl.loop(0, grid_count)
        def _(n):
            value = pair_ref[i, 0, n].astype(f32)
            for d in range(1, nx):
                value = value + peer_ref[i, d, n].astype(f32)
            total_ref[n, :, i * width : (i + 1) * width] = value.astype(bf16)

    g_copies = []
    for d in range(1, grid_count):
        target = lax.rem(g + d, grid_count)
        copy = remote(
            total_ref.at[target], out_ref.at[g], gs.at[d], gr.at[d], g_peers[d - 1]
        )
        copy.start()
        g_copies.append(copy)
    out_ref[g] = total_ref[g]

    @pl.when(is_owner)
    def _():
        for i in range(len(x_peers + c_peers)):
            remote(rows_ref, rows_ref, es.at[i], er.at[0, 0], right).wait_send()
        own.wait()

    if nc == 2:

        @pl.when(jnp.logical_and(in_column, jnp.logical_not(is_owner)))
        def _():
            remote(rows_ref, rows_ref, es.at[nx - 1], er.at[0, 0], right).wait_send()

        waits_rows = jnp.logical_not(in_column)
    else:
        waits_rows = jnp.logical_not(is_owner)

    @pl.when(waits_rows)
    def _():
        for k in steps:

            @pl.when(present(k))
            def _():
                for d in range(ny):
                    spot = rows_ref.at[source(k, d)]
                    remote(spot, spot, es.at[0], er.at[d, k], right).wait_recv()

    for k in steps:

        @pl.when(present(k))
        def _():
            if k == 0 or k % 2:

                @pl.when(has_right)
                def _():
                    along(k, True).wait_send()

            if k == 0 or k % 2 == 0:

                @pl.when(has_left)
                def _():
                    along(k, False).wait_send()

            for d in range(1, ny):
                across(k, d).wait_send()

    for i in range(chunks):
        for d in range(nx):
            if nc == 2:
                core_copy(i, d).wait_send()
            if d:
                pair_copy(i, d).wait_send()
    for copy in g_copies:
        copy.wait()


def smem():
    return pl.BlockSpec(memory_space=pltpu.SMEM)


def front(sig_blocks, values, density, block_size, grid_count, tile_count):
    batch, cols = values.shape
    rows = density.shape[0]
    nz, ny = grid_split(grid_count)
    nx, nc = tile_split(tile_count)
    slab = batch // tile_count
    width = min(rows, 512)
    chunks = rows // width
    dma = pltpu.SemaphoreType.DMA
    return pl.pallas_call(
        functools.partial(front_kernel, block_size, grid_count, tile_count),
        out_shape=(
            jax.ShapeDtypeStruct((grid_count, slab, rows), bf16),
            jax.ShapeDtypeStruct((grid_count, batch, rows), bf16),
        ),
        in_specs=[smem(), vmem(), pl.BlockSpec(memory_space=pl.ANY)],
        out_specs=(vmem(), vmem()),
        scratch_shapes=[
            pltpu.VMEM((batch, cols), bf16),
            pltpu.VMEM((grid_count, batch, cols), bf16),
            pltpu.VMEM((rows, cols), bf16),
            pltpu.VMEM((chunks, grid_count, nx, nc, slab, width), bf16),
            pltpu.VMEM((chunks, grid_count, nx, slab, width), bf16),
            pltpu.VMEM((chunks, nx, grid_count, slab, width), bf16),
            pltpu.VMEM((chunks, nx, grid_count, slab, width), bf16),
            pltpu.VMEM((grid_count, slab, rows), bf16),
            dma((2, nz)),
            dma((2, nz)),
            dma((ny, 2 * nz)),
            dma((ny, 2 * nz)),
            dma((nx,)),
            dma((ny, 2 * nz)),
            dma,
            dma((chunks,)),
            dma((chunks, nx)),
            dma((chunks, nx)),
            dma((chunks, nx)),
            dma((chunks, nx)),
            dma((grid_count,)),
            dma((grid_count,)),
        ],
        compiler_params=params(0),
    )(sig_blocks, values, density)


def finish_kernel(
    grid_count,
    tile_count,
    pot_ref,
    lmo_hbm,
    domain_ref,
    all_ref,
    lmo_ref,
    got_ref,
    flat_ref,
    send_ref,
    part_ref,
    own_ref,
    lmo_sem,
    vs,
    vr,
    ws,
    wr,
    gs,
    gr,
):
    g, t = lax.axis_index("grid"), lax.axis_index("tile")
    load = pltpu.make_async_copy(lmo_hbm, lmo_ref, lmo_sem)
    load.start()
    t_peers = [(g, lax.rem(t + d, tile_count)) for d in range(1, tile_count)]
    g_peers = [(lax.rem(g + d, grid_count), t) for d in range(1, grid_count)]
    greet(t_peers + g_peers)
    cols = got_ref.shape[1]
    strips = domain_ref.shape[0]
    slab = pot_ref.shape[1]
    block = pot_ref.shape[2]
    strip = own_ref.shape[1]

    v_copies = []
    for d in range(1, tile_count):
        target = lax.rem(t + d, tile_count)
        copy = remote(
            pot_ref.at[pl.ds(target * cols, cols)],
            got_ref.at[t],
            vs.at[d],
            vr.at[d],
            t_peers[d - 1],
        )
        copy.start()
        v_copies.append(copy)
    got_ref[t] = pot_ref[pl.ds(t * cols, cols)]
    flags = [[listed(domain_ref, s, t * cols + m) for m in range(cols)] for s in range(strips)]
    for copy in v_copies:
        copy.wait()
    for i in range(tile_count):
        for m in range(cols):
            flat_ref[m, i * slab : (i + 1) * slab, :] = got_ref[i, m].astype(f32)
    load.wait()
    width = lmo_ref.shape[1] // strips
    per_tile = strips // tile_count
    for s in range(strips):
        lanes = slice(s * width, (s + 1) * width)
        total = None
        for m in range(cols):
            term = flags[s][m] * jnp.dot(
                flat_ref[m].astype(bf16),
                lmo_ref[m * block : (m + 1) * block, lanes],
                preferred_element_type=f32,
            )
            total = term if total is None else total + term
        first = s % per_tile * width
        send_ref[s // per_tile, :, first : first + width] = total.astype(bf16)
    w_copies = []
    for d in range(1, tile_count):
        target = lax.rem(t + d, tile_count)
        copy = remote(
            send_ref.at[target], part_ref.at[d], ws.at[d], wr.at[d], t_peers[d - 1]
        )
        copy.start()
        w_copies.append(copy)
    total = send_ref[t].astype(f32)
    for d, copy in enumerate(w_copies):
        copy.wait()
        total = total + part_ref[d + 1].astype(f32)
    own_ref[...] = total.astype(bf16)
    g_copies = []
    for d in range(1, grid_count):
        copy = remote(own_ref, all_ref.at[g], gs.at[d], gr.at[d], g_peers[d - 1])
        copy.start()
        g_copies.append(copy)
    all_ref[g] = own_ref[...]
    for copy in g_copies:
        copy.wait()


def finish(potential, lmo_coeffs, domain_blocks, batch, grid_count, tile_count):
    blocks, slab, block = potential.shape
    cols = blocks // tile_count
    total = lmo_coeffs.shape[1]
    strip = total // tile_count
    dma = pltpu.SemaphoreType.DMA
    return pl.pallas_call(
        functools.partial(finish_kernel, grid_count, tile_count),
        out_shape=jax.ShapeDtypeStruct((grid_count, batch, strip), bf16),
        in_specs=[vmem(), pl.BlockSpec(memory_space=pl.ANY), smem()],
        out_specs=vmem(),
        scratch_shapes=[
            pltpu.VMEM(lmo_coeffs.shape, bf16),
            pltpu.VMEM((tile_count, cols, slab, block), bf16),
            pltpu.VMEM((cols, batch, block), f32),
            pltpu.VMEM((tile_count, batch, strip), bf16),
            pltpu.VMEM((tile_count, batch, strip), bf16),
            pltpu.VMEM((batch, strip), bf16),
            dma,
            dma((tile_count,)),
            dma((tile_count,)),
            dma((tile_count,)),
            dma((tile_count,)),
            dma((grid_count,)),
            dma((grid_count,)),
        ],
        compiler_params=params(2),
    )(potential, lmo_coeffs, domain_blocks)


def shards(
    point_values,
    sig_blocks,
    density,
    coulomb_core,
    screen_mask,
    ao_centers,
    ao_widths,
    point_coords,
    lmo_coeffs,
    domain_blocks,
):
    grid_count = lax.axis_size("grid")
    tile_count = lax.axis_size("tile")
    panel = lax.axis_index("tile")
    own_rows, own_cols = density.shape
    points = point_values.shape[0]
    block_size = coulomb_core.shape[0]
    total_aos = ao_widths.shape[0]
    all_blocks = total_aos // block_size
    slab = points // tile_count
    block_ids = jnp.arange(all_blocks, dtype=jnp.int32)
    named = jnp.any(sig_blocks[0][:, None] == block_ids[None, :], axis=0)
    summed, row_values = front(
        sig_blocks, point_values, density, block_size, grid_count, tile_count
    )
    row_blocks = own_rows // block_size
    term = summed.astype(f32).reshape(grid_count, slab, row_blocks, block_size)
    term = jnp.transpose(term, (0, 2, 1, 3)).reshape(all_blocks, slab, block_size)
    coords = lax.dynamic_slice_in_dim(point_coords, panel * slab, slab, 1)
    offsets = (
        ao_centers.reshape(3, all_blocks, 1, block_size) - coords.reshape(3, 1, slab, 1)
    )
    coefficient = 1.0 / jnp.sqrt(
        jnp.sum(offsets * offsets, axis=0) + ao_widths.reshape(all_blocks, 1, block_size)
    )
    scaled = coefficient * named.astype(f32)[:, None, None]
    weighted = (scaled * term).astype(bf16)
    screened = jnp.einsum(
        "kj,jpa->kpa", screen_mask.astype(bf16), weighted, preferred_element_type=f32
    ).astype(bf16)
    mixed = jnp.einsum(
        "kpc,ac->kpa", screened, coulomb_core, preferred_element_type=f32
    )
    potential = (scaled * mixed).astype(bf16)
    weights = finish(potential, lmo_coeffs, domain_blocks, points, grid_count, tile_count)
    return lax.dot_general(
        weights.reshape(grid_count * points, weights.shape[2]),
        row_values.reshape(grid_count * points, own_rows),
        (((0,), (0,)), ((), ())),
        preferred_element_type=f32,
    ).astype(bf16)


def solution(mesh):
    in_specs = (
        P("grid", "tile"),
        P("grid", None),
        P("grid", "tile"),
        P(),
        P(),
        P(),
        P(),
        P(None, "grid"),
        P("tile", None),
        P(),
    )
    out_specs = P("tile", "grid")
    return jax.shard_map(shards, mesh=mesh, in_specs=in_specs, out_specs=out_specs, check_vma=False)
```
